32 devices in a mesh: groups: 2 (over y), hidden: 4 (over z), width: 2 (over x), rep: 2 (over core).
Axes of the slice: x: 2, y: 2, z: 4, core: 2. Of those that a mesh axis runs over, the one named last changes fastest.
Arguments:
- tokens: bfloat16 [1024, 5120], P(('groups', 'rep'), 'width'), parts along dimension 0, may hold values from -6 to 6
- w_gate: bfloat16 [5120, 13824], P(('width', 'rep'), 'hidden'), may hold values from -0.078125 to 0.078125
- w_up: bfloat16 [5120, 13824], P(('width', 'rep'), 'hidden'), may hold values from -0.078125 to 0.078125
- w_down: bfloat16 [13824, 5120], P('hidden', ('width', 'rep')), may hold values from -0.0546875 to 0.0546875
- keep_a: int32 [128], P('hidden'), may hold values from 0 to 1, as said below
- keep_b: int32 [128], P('hidden'), may hold values from 0 to 1, as said below
Outputs:
- grad_gate_a: bfloat16 [5120, 20736], P(('width', 'rep'), ('groups', 'hidden')), parts along dimension 1
- grad_up_a: bfloat16 [5120, 20736], P(('width', 'rep'), ('groups', 'hidden')), parts along dimension 1
- grad_down_a: bfloat16 [20736, 5120], P(('groups', 'hidden'), ('width', 'rep')), parts along dimension 0
- grad_gate_b: bfloat16 [5120, 13824], P(('width', 'rep'), ('groups', 'hidden')), parts along dimension 1
- grad_up_b: bfloat16 [5120, 13824], P(('width', 'rep'), ('groups', 'hidden')), parts along dimension 1
- grad_down_b: bfloat16 [13824, 5120], P(('groups', 'hidden'), ('width', 'rep')), parts along dimension 0
- losses: float32 [4], P('groups'), parts along dimension 0
The draws below stay inside these ranges and needn't reach their ends.
There are 2 independent parts, one for each index of `groups`. The reference program is written for one: setup_inputs(seed, part) draws one part's arguments, and reference() takes and returns one part's arrays. A program takes and returns all parts, laid end to end along the dimension named above; an argument that names none is the same for every part. Nothing has to cross between parts.
Inputs may be any that keep to these rules, and one draw needn't show every extreme that they name: `keep_a`: 0 or 1 for each block of 108 units of the parent; 6912 units are kept in all; each shard of 32 consecutive blocks keeps at most 24, and some shard keeps exactly 24. `keep_b`: 0 or 1 for each block of 108 units of the parent; 3456 units are kept in all; each shard of 32 consecutive blocks keeps at most 16, and some shard keeps exactly 16.
All inputs are finite; a program needn't handle non-finite values.
Results may differ from the reference program's by a relative error of at most 0.0075.
Values may be sent and summed in bfloat16 or wider, within the bound.
A program may use at most 192 MiB of HBM per device.

```python
import jax
import jax.numpy as jnp

D = 5120
FF = 13824
BLOCK = 108
TOKENS = 512
SHARD_BLOCKS = 32
SLOT_A = 24
SLOT_B = 16


def keep_table(key, middle, spread, salt_value):
    shards = FF // BLOCK // SHARD_BLOCKS
    shard_order = jax.random.permutation(jax.random.fold_in(key, salt_value), shards)
    heavy_shards = (shard_order < shards // 2).astype(jnp.int32)
    counts = middle - spread + 2 * spread * heavy_shards
    scores = jax.random.randint(jax.random.fold_in(key, salt_value + 1), (shards, SHARD_BLOCKS), 0, 1 << 20) * SHARD_BLOCKS
    scores = scores + jnp.arange(SHARD_BLOCKS, dtype=jnp.int32)[None, :]
    ranking = jnp.argsort(jnp.argsort(scores, axis=1), axis=1)
    return (ranking < counts[:, None]).astype(jnp.int32).reshape(-1)


def draw_keep_a(key, part):
    return keep_table(key, SHARD_BLOCKS // 2, SHARD_BLOCKS // 4, 101)


def draw_keep_b(key, part):
    return keep_table(key, SHARD_BLOCKS // 4, SHARD_BLOCKS // 4, 203)


def block_scale(stream_key, dims, cuts, smallest, top_value):
    gain = 1.0
    for dim, blocks in cuts:
        draws = jax.random.uniform(jax.random.fold_in(jax.random.fold_in(stream_key, 6), dim), (blocks,), jnp.float32, smallest / len(cuts), top_value / len(cuts))
        gain = gain * jnp.repeat(jnp.exp(draws), dims[dim] // blocks).reshape((-1,) + (1,) * (len(dims) - 1 - dim))
    return gain


def noise(rng, shape, scale, reach, split=(), kind=jnp.bfloat16):
    entries = jax.random.normal(rng, shape, jnp.float32) * scale
    if len(split) > 0:
        entries = block_scale(rng, shape, split, -0.22, 0.18) * entries
    return jnp.clip(entries, min=-reach, max=reach).astype(kind)


def setup_inputs(seed: int = 0, part: int = 0) -> dict:
    key_list = jax.random.split(jax.random.key(seed), 7)
    own_keys = jax.random.split(jax.random.fold_in(key_list[6], part), 7)
    tokens = noise(own_keys[0], (TOKENS, D), 1.0, 6.0, ((0, 2), (1, 2)))
    w_gate = noise(key_list[1], (D, FF), D ** -0.5, 0.078125, ((0, 4), (1, 4)))
    w_up = noise(key_list[2], (D, FF), D ** -0.5, 0.078125, ((0, 4), (1, 4)))
    w_down = noise(key_list[3], (FF, D), FF ** -0.5, 0.0546875, ((0, 4), (1, 4)))
    keep_a = draw_keep_a(jax.random.fold_in(key_list[6], 71), part)
    keep_b = draw_keep_b(jax.random.fold_in(key_list[6], 71), part)
    return dict(tokens=tokens, w_gate=w_gate, w_up=w_up, w_down=w_down, keep_a=keep_a, keep_b=keep_b)


def slot_columns(keep_mask, slot_count):
    groups = keep_mask.reshape(-1, SHARD_BLOCKS)
    ranking = (jnp.cumsum(groups, axis=1) - 1).astype(jnp.int32)
    slot_ids = jnp.arange(slot_count, dtype=jnp.int32)
    matches = groups[:, None, :] * (ranking[:, None, :] == slot_ids[None, :, None]).astype(jnp.int32)
    positions = jnp.arange(SHARD_BLOCKS, dtype=jnp.int32)
    offsets = (jnp.arange(groups.shape[0], dtype=jnp.int32) * SHARD_BLOCKS)[:, None]
    block_index = (jnp.sum(matches * positions[None, None, :], axis=2) + offsets).astype(jnp.int32)
    block_live = jnp.sum(matches, axis=2).astype(jnp.int32)
    columns = (block_index[:, :, None] * BLOCK + jnp.arange(BLOCK, dtype=jnp.int32)[None, None, :]).reshape(-1).astype(jnp.int32)
    live = jnp.broadcast_to(block_live[:, :, None], block_live.shape + (BLOCK,)).reshape(-1)
    return columns, live


def reference(tokens, w_gate, w_up, w_down, keep_a, keep_b):
    gate_value = jnp.dot(tokens, w_gate, preferred_element_type=jnp.float32)
    up_value = jnp.dot(tokens, w_up, preferred_element_type=jnp.float32)
    sigmoid_term = jax.nn.sigmoid(gate_value)
    activation = jax.nn.silu(gate_value)
    slope_term = sigmoid_term * (1.0 + gate_value * (1.0 - sigmoid_term))
    hidden = (activation * up_value).astype(jnp.bfloat16)
    outputs = []
    loss_list = []
    for keep_mask, slot_count in ((keep_a, SLOT_A), (keep_b, SLOT_B)):
        dropped = (1 - jnp.repeat(keep_mask, BLOCK)).astype(jnp.bfloat16)
        difference = -jnp.dot(hidden * dropped[None, :], w_down, preferred_element_type=jnp.float32)
        loss_list.append(jnp.sum(difference * difference) / (TOKENS * D))
        errors = difference.astype(jnp.bfloat16)
        columns, live = slot_columns(keep_mask, slot_count)
        live_float = live.astype(jnp.float32)
        hidden_slot = jnp.take(hidden, columns, axis=1) * live.astype(jnp.bfloat16)[None, :]
        grad_down = jnp.dot(hidden_slot.T, errors, preferred_element_type=jnp.float32).astype(jnp.bfloat16)
        back_total = jnp.dot(errors, jnp.take(w_down, columns, axis=0).T, preferred_element_type=jnp.float32)
        delta_gate = (back_total * jnp.take(up_value, columns, axis=1) * jnp.take(slope_term, columns, axis=1) * live_float[None, :]).astype(jnp.bfloat16)
        delta_up = (back_total * jnp.take(activation, columns, axis=1) * live_float[None, :]).astype(jnp.bfloat16)
        grad_gate = jnp.dot(tokens.T, delta_gate, preferred_element_type=jnp.float32).astype(jnp.bfloat16)
        grad_up = jnp.dot(tokens.T, delta_up, preferred_element_type=jnp.float32).astype(jnp.bfloat16)
        outputs.append((grad_gate, grad_up, grad_down))
    losses = jnp.stack(loss_list).astype(jnp.float32)
    return (outputs[0][0], outputs[0][1], outputs[0][2], outputs[1][0], outputs[1][1], outputs[1][2], losses)
```

```python
import functools

import jax
import jax.numpy as jnp
from jax import lax
from jax.experimental import pallas as pl
from jax.experimental.pallas import tpu as pltpu
from jax.sharding import PartitionSpec as P


D = 5120
BLOCK = 108


def block_slots(keep_mask, slot_count):
    positions = jnp.arange(keep_mask.shape[0], dtype=jnp.int32)
    ranking = jnp.cumsum(keep_mask) - 1
    slot_ids = jnp.arange(slot_count, dtype=jnp.int32)
    matches = keep_mask[None, :] * (ranking[None, :] == slot_ids[:, None]).astype(jnp.int32)
    block_index = jnp.sum(matches * positions[None, :], axis=1)
    block_live = jnp.sum(matches, axis=1)
    return (block_index, block_live)


def pick_blocks(matrix, block_index, block_live, dim_axis):
    if dim_axis == 1:
        grouped = matrix.reshape(matrix.shape[0], -1, BLOCK)
        picked = jnp.take(grouped, block_index, axis=1) * block_live[None, :, None].astype(
            matrix.dtype
        )
        return picked.reshape(matrix.shape[0], -1)
    grouped = matrix.reshape(-1, BLOCK, matrix.shape[1])
    picked = jnp.take(grouped, block_index, axis=0) * block_live[:, None, None].astype(matrix.dtype)
    return picked.reshape(-1, matrix.shape[1])


def per_device(tokens, w_gate, w_up, w_down, keep_a, keep_b):
    gathered = lax.all_to_all(tokens, "rep", split_axis=1, concat_axis=0, tiled=True)
    part_gate = jnp.dot(gathered, w_gate, preferred_element_type=jnp.float32)
    part_up = jnp.dot(gathered, w_up, preferred_element_type=jnp.float32)
    gate_value, up_value = lax.psum((part_gate, part_up), ("width", "rep"))
    sigmoid_term = jax.nn.sigmoid(gate_value)
    activation = gate_value * sigmoid_term
    slope_term = sigmoid_term * (1.0 + gate_value * (1.0 - sigmoid_term))
    hidden = (activation * up_value).astype(jnp.bfloat16)
    shard_blocks = keep_a.shape[0]
    variant_plans = ((keep_a, 3 * shard_blocks // 4), (keep_b, shard_blocks // 2))
    differences = jnp.stack(
        [
            -jnp.dot(
                hidden * (1 - jnp.repeat(keep_mask, BLOCK)).astype(jnp.bfloat16)[None, :],
                w_down,
                preferred_element_type=jnp.float32,
            )
            for keep_mask, slot_count in variant_plans
        ]
    )
    scale_count = gathered.shape[0] * D
    totals = lax.psum(differences, "hidden")
    squares = jnp.sum(totals * totals, axis=(1, 2))
    losses = lax.psum(squares, ("width", "rep")) / scale_count
    errors = totals.astype(jnp.bfloat16)
    slot_plans = [block_slots(keep_mask, slot_count) for keep_mask, slot_count in variant_plans]
    back_terms = [
        jnp.einsum(
            "td,fd->tf",
            errors[variant],
            pick_blocks(w_down, slot_plans[variant][0], slot_plans[variant][1], 0),
            preferred_element_type=jnp.float32,
        )
        for variant in range(2)
    ]
    back_a, back_b = lax.psum((back_terms[0], back_terms[1]), ("width", "rep"))
    results = []
    for variant, back_total in ((0, back_a), (1, back_b)):
        block_index, block_live = slot_plans[variant]
        keep_mask = variant_plans[variant][0]
        up_slot = pick_blocks(up_value, block_index, block_live, 1)
        slope_slot = pick_blocks(slope_term, block_index, block_live, 1)
        act_slot = pick_blocks(activation, block_index, block_live, 1)
        hidden_slot = pick_blocks(hidden, block_index, block_live, 1)
        delta_gate = (back_total * up_slot * slope_slot).astype(jnp.bfloat16)
        delta_up = (back_total * act_slot).astype(jnp.bfloat16)
        grad_gate = jnp.einsum(
            "td,tf->df", gathered, delta_gate, preferred_element_type=jnp.float32
        )
        grad_up = jnp.einsum("td,tf->df", gathered, delta_up, preferred_element_type=jnp.float32)
        grad_down = jnp.einsum(
            "tf,td->fd", hidden_slot, errors[variant], preferred_element_type=jnp.float32
        )
        results.append(
            (
                grad_gate.astype(jnp.bfloat16),
                grad_up.astype(jnp.bfloat16),
                grad_down.astype(jnp.bfloat16),
            )
        )
    return (
        results[0][0],
        results[0][1],
        results[0][2],
        results[1][0],
        results[1][1],
        results[1][2],
        losses,
    )


MESH = pl.DeviceIdType.MESH
VMEM_LIMIT = 63 << 20


def nt(a, b):
    return lax.dot_general(a, b, (((1,), (1,)), ((), ())), preferred_element_type=jnp.float32)


def nn(a, b):
    return jnp.dot(a, b, preferred_element_type=jnp.float32)


def forward_kernel(
    chunks, block,
    tok_hbm, wg_hbm, wu_hbm, wd_hbm, mask_ref,
    err_hbm, hid_hbm, act_hbm, fac_hbm, tok_out, sq_ref,
    tok, wgb, wub, wd, part, stage, ring, xs, xr, hid, lhs, zp, zs, zr, errs,
    tok_s, tok_r, w_sem, wd_sem, st_s, ring_r, x_s, x_r, hid_s, hid_r, z_s, z_r, keep_s, err_s,
):
    n = lax.axis_size("hidden")
    z, wide, core = lax.axis_index("hidden"), lax.axis_index("width"), lax.axis_index("rep")
    depth, units = wg_hbm.shape
    half = tok_hbm.shape[0]
    blocks = units // block
    partner, across = {"rep": 1 - core}, {"width": 1 - wide}

    def local(src, dst, sem):
        return pltpu.make_async_copy(src, dst, sem)

    def remote(src, dst, ssem, rsem, peer):
        return pltpu.make_async_remote_copy(
            src, dst, ssem, rsem, device_id=peer, device_id_type=MESH
        )

    def weights(j):
        lanes = pl.ds(pl.multiple_of(j * block, 128), block)
        slot = lax.rem(j, 2)
        return (
            local(wg_hbm.at[:, lanes], wgb.at[slot], w_sem.at[0, slot]),
            local(wu_hbm.at[:, lanes], wub.at[slot], w_sem.at[1, slot]),
        )

    for j in range(2):
        for copy in weights(j):
            copy.start()
    mine = local(
        tok_hbm.at[:, pl.ds(pl.multiple_of(core * depth, 128), depth)], tok.at[0], wd_sem
    )
    mine.start()
    load_down = local(wd_hbm, wd, wd_sem)

    barrier = pltpu.get_barrier_semaphore()
    pl.semaphore_signal(barrier, inc=1, device_id=partner, device_id_type=MESH)
    pl.semaphore_signal(barrier, inc=1, device_id=across, device_id_type=MESH)

    @pl.when(z > 0)
    def _():
        pl.semaphore_signal(barrier, inc=1, device_id={"hidden": z - 1}, device_id_type=MESH)

    @pl.when(z < n - 1)
    def _():
        pl.semaphore_signal(barrier, inc=1, device_id={"hidden": z + 1}, device_id_type=MESH)

    @pl.when((z == 0) | (z == n - 1))
    def _():
        pl.semaphore_wait(barrier, 3)

    @pl.when((z > 0) & (z < n - 1))
    def _():
        pl.semaphore_wait(barrier, 4)

    give = remote(
        tok_hbm.at[:, pl.ds(pl.multiple_of((1 - core) * depth, 128), depth)],
        tok.at[1], tok_s, tok_r, partner,
    )
    give.start()
    sq_ref[...] = jnp.zeros_like(sq_ref)
    mine.wait()
    give.wait()
    load_down.start()
    keep_tok = local(tok, tok_out, tok_s)
    keep_tok.start()

    def push(j):
        return remote(
            stage.at[lax.rem(j, 2)], ring.at[lax.rem(j, 4)],
            st_s.at[lax.rem(j, 2)], ring_r.at[lax.rem(j, 4)], partner,
        )

    first = chunks[0][1]

    def cross_block(j):
        lanes = pl.ds(pl.multiple_of(j * block, 128), block)
        return remote(
            xs.at[:, pl.ds(0, first), lanes], xr.at[:, pl.ds(0, first), lanes],
            x_s.at[0], x_r.at[0], across,
        )

    def cross(c):
        rows = pl.ds(*chunks[c])
        return remote(xs.at[:, rows, :], xr.at[:, rows, :], x_s.at[c], x_r.at[c], across)

    def take(j):
        lanes = pl.ds(pl.multiple_of(j * block, 128), block)
        slot = lax.rem(j, 4)
        push(j).wait_recv()
        for i in range(2):
            total = part[i, :, lanes] + ring[slot, i]
            part[i, :, lanes] = total
            xs[i, :, lanes] = total.astype(jnp.bfloat16)
        cross_block(j).start()

    def step(j, carry):
        for copy in weights(j):
            copy.wait()
        slot = lax.rem(j, 2)
        lanes = pl.ds(pl.multiple_of(j * block, 128), block)

        @pl.when(j >= 2)
        def _():
            push(j).wait_send()

        stage[slot, 0] = nn(tok[1], wgb[slot])
        stage[slot, 1] = nn(tok[1], wub[slot])
        push(j).start()

        @pl.when(j >= 1)
        def _():
            take(j - 1)

        part[0, :, lanes] = nn(tok[0], wgb[slot])
        part[1, :, lanes] = nn(tok[0], wub[slot])

        @pl.when(j + 2 < blocks)
        def _():
            for copy in weights(j + 2):
                copy.start()

        return carry

    lax.fori_loop(0, blocks, step, 0)
    take(blocks - 1)
    for c in range(1, len(chunks)):
        cross(c).start()
    for j in (blocks - 2, blocks - 1):
        push(j).wait_send()
    load_down.wait()

    def swap_hidden(c):
        rows = pl.ds(*chunks[c])
        return remote(hid.at[0, rows], hid.at[1, rows], hid_s.at[c], hid_r.at[c], partner)

    def keep_out(c):
        rows = pl.ds(*chunks[c])
        return (
            local(part.at[0, rows], act_hbm.at[rows], keep_s.at[0, c]),
            local(part.at[1, rows], fac_hbm.at[rows], keep_s.at[1, c]),
        )

    def activate(c):
        start, count = chunks[c]
        rows = pl.ds(start, count)
        cross(c).wait_recv()

        def lane_block(j, carry):
            lanes = pl.ds(pl.multiple_of(j * block, 128), block)
            gate = part[0, rows, lanes] + xr[0, rows, lanes].astype(jnp.float32)
            up = part[1, rows, lanes] + xr[1, rows, lanes].astype(jnp.float32)
            sigmoid = jax.nn.sigmoid(gate)
            act = gate * sigmoid
            hid[0, rows, lanes] = (act * up).astype(jnp.bfloat16)
            part[0, rows, lanes] = act
            part[1, rows, lanes] = up * (sigmoid * (1.0 + gate * (1.0 - sigmoid)))
            return carry

        lax.fori_loop(0, blocks, lane_block, 0)
        swap_hidden(c).start()
        for copy in keep_out(c):
            copy.start()

    def differ(c):
        start, count = chunks[c]
        rows = pl.ds(start, count)
        swap_hidden(c).wait_recv()

        def masked(j, carry):
            lanes = pl.ds(pl.multiple_of(j * block, 128), block)
            for side in range(2):
                value = hid[side, rows, lanes]
                for k in range(2):
                    drop = mask_ref[k : k + 1, lanes].astype(jnp.bfloat16)
                    lhs[pl.ds((2 * k + side) * count, count), lanes] = value * drop
            return carry

        lax.fori_loop(0, blocks, masked, 0)

        def columns(j, carry):
            lanes = pl.ds(pl.multiple_of(j * 256, 128), 256)
            zp[pl.ds(4 * start, 4 * count), lanes] = nn(lhs[pl.ds(0, 4 * count), :], wd[:, lanes])
            return carry

        lax.fori_loop(0, depth // 256, columns, 0)

    def z_copy(c, d, q):
        start, count = chunks[c]
        rows = pl.ds(pl.multiple_of(4 * start + q * count, 16), count)
        peer = {"hidden": z + 1 - 2 * d}
        return remote(zs.at[d, rows], zr.at[d, rows], z_s.at[c, d, q], z_r.at[c, d, q], peer)

    def has_up(d):
        return ((d == 0) & (z > 0)) | ((d == 1) & (z < n - 1))

    def has_down(d):
        return ((d == 0) & (z < n - 1)) | ((d == 1) & (z > 0))

    def hop(c, d, q):
        start, count = chunks[c]
        rows = pl.ds(pl.multiple_of(4 * start + q * count, 16), count)

        @pl.when(has_up(d))
        def _():
            z_copy(c, d, q).wait_recv()

        @pl.when(has_up(d) & has_down(d))
        def _():
            total = zp[rows, :] + zr[d, rows, :].astype(jnp.float32)
            zs[d, rows, :] = total.astype(jnp.bfloat16)

        @pl.when(has_down(d) & jnp.logical_not(has_up(d)))
        def _():
            zs[d, rows, :] = zp[rows, :].astype(jnp.bfloat16)

        @pl.when(has_down(d))
        def _():
            z_copy(c, d, q).start()

    def err_out(c, q):
        start, count = chunks[c]
        rows = pl.ds(pl.multiple_of(4 * start + q * count, 16), count)
        return local(errs.at[rows], err_hbm.at[q, pl.ds(start, count)], err_s.at[c, q])

    def finish(c, q):
        start, count = chunks[c]
        rows = pl.ds(pl.multiple_of(4 * start + q * count, 16), count)

        def settle(total):
            errs[rows, :] = total.astype(jnp.bfloat16)
            square = total * total
            folded = square[0:8]
            for i in range(8, count, 8):
                folded = folded + square[i : i + 8]
            narrow = folded[:, 0:128]
            for i in range(128, depth, 128):
                narrow = narrow + folded[:, i : i + 128]
            k = q // 2
            sq_ref[k] = sq_ref[k] + narrow

        @pl.when(z == 0)
        def _():
            settle(zp[rows, :] + zr[1, rows, :].astype(jnp.float32))

        @pl.when(z == n - 1)
        def _():
            settle(zp[rows, :] + zr[0, rows, :].astype(jnp.float32))

        @pl.when((z > 0) & (z < n - 1))
        def _():
            settle(
                zp[rows, :]
                + (zr[0, rows, :].astype(jnp.float32) + zr[1, rows, :].astype(jnp.float32))
            )

        err_out(c, q).start()

    early = (2 * z) // n
    late = 1 - early
    edge = (z == 0) | (z == n - 1)
    last = len(chunks) - 1

    def each(*actions):
        def piece(q, carry):
            for action, c, args in actions:
                action(c, *args, q)
            return carry

        lax.fori_loop(0, 4, piece, 0)

    for c in range(len(chunks)):
        activate(c)
        differ(c)

        @pl.when(edge)
        def _(c=c):
            each((hop, c, (early,)))
            if c > 1:
                each((hop, c - 2, (late,)), (finish, c - 2, ()))

        @pl.when(jnp.logical_not(edge))
        def _(c=c):
            behind = ((hop, c - 1, (late,)), (finish, c - 1, ())) if c > 0 else ()
            each(*behind, (hop, c, (early,)))

    @pl.when(edge)
    def _():
        each((hop, last - 1, (late,)), (finish, last - 1, ()))

    each((hop, last, (late,)), (finish, last, ()))

    keep_tok.wait()
    for side in range(2):
        local(hid.at[side], hid_hbm.at[side], w_sem.at[0, side]).start()
    for side in range(2):
        local(hid.at[side], hid_hbm.at[side], w_sem.at[0, side]).wait()
    for c in range(len(chunks)):
        cross(c).wait_send()
        swap_hidden(c).wait_send()
        for copy in keep_out(c):
            copy.wait()

        def drain(q, carry, c=c):
            err_out(c, q).wait()
            for d in range(2):
                @pl.when(has_down(d))
                def _():
                    z_copy(c, d, q).wait_send()
            return carry

        lax.fori_loop(0, 4, drain, 0)


def forward_call(tokens, w_gate, w_up, w_down, masks):
    half, (depth, units) = tokens.shape[0], w_gate.shape
    block = 384 if units % 384 == 0 else 128
    counts = [half * part // 16 for part in (4, 4, 3, 3, 2)]
    chunks = tuple((sum(counts[:i]), count) for i, count in enumerate(counts))
    parts = len(chunks)
    bf, f32 = jnp.bfloat16, jnp.float32
    anywhere = pl.BlockSpec(memory_space=pl.ANY)
    vmem = pl.BlockSpec(memory_space=pltpu.VMEM)
    dma = pltpu.SemaphoreType.DMA
    return pl.pallas_call(
        functools.partial(forward_kernel, chunks, block),
        out_shape=(
            jax.ShapeDtypeStruct((4, half, depth), bf),
            jax.ShapeDtypeStruct((2, half, units), bf),
            jax.ShapeDtypeStruct((half, units), f32),
            jax.ShapeDtypeStruct((half, units), f32),
            jax.ShapeDtypeStruct((2, half, depth), bf),
            jax.ShapeDtypeStruct((2, 8, 128), f32),
        ),
        in_specs=[anywhere] * 4 + [vmem],
        out_specs=(anywhere,) * 5 + (vmem,),
        scratch_shapes=[
            pltpu.VMEM((2, half, depth), bf),
            pltpu.VMEM((2, depth, block), bf),
            pltpu.VMEM((2, depth, block), bf),
            pltpu.VMEM((units, depth), bf),
            pltpu.VMEM((2, half, units), f32),
            pltpu.VMEM((2, 2, half, block), f32),
            pltpu.VMEM((4, 2, half, block), f32),
            pltpu.VMEM((2, half, units), bf),
            pltpu.VMEM((2, half, units), bf),
            pltpu.VMEM((2, half, units), bf),
            pltpu.VMEM((4 * max(counts), units), bf),
            pltpu.VMEM((4 * half, depth), f32),
            pltpu.VMEM((2, 4 * half, depth), bf),
            pltpu.VMEM((2, 4 * half, depth), bf),
            pltpu.VMEM((4 * half, depth), bf),
            dma, dma, dma((2, 2)), dma, dma((2,)), dma((4,)),
            dma((parts,)), dma((parts,)), dma((parts,)), dma((parts,)),
            dma((parts, 2, 4)), dma((parts, 2, 4)), dma((2, parts)), dma((parts, 4)),
        ],
        compiler_params=pltpu.CompilerParams(
            collective_id=0, has_side_effects=True, vmem_limit_bytes=VMEM_LIMIT
        ),
    )(tokens, w_gate, w_up, w_down, masks)


def backward_kernel(
    slots,
    start_ref, live_ref, err_hbm, wd_hbm, act_hbm, fac_hbm, hid_hbm, sq_ref,
    dga_hbm, dua_hbm, ha_hbm, dgb_hbm, dub_hbm, hb_hbm, loss_ref,
    wd, err, bt, give, got, own, xs, xr, nat, act_t, fac_t, hidb, outs, hout,
    sq_core, sq_chip, sq_all,
    in_s, give_s, give_r, x_s, x_r, own_s, far_s, far_r, h_s, l_s, l_r, z_s, z_r,
):
    n = lax.axis_size("hidden")
    z, wide, core = lax.axis_index("hidden"), lax.axis_index("width"), lax.axis_index("rep")
    units, depth = wd_hbm.shape
    half = act_hbm.shape[0]
    pairs = half // 128
    slots_a, slots_b = slots
    rows_a, rows = slots_a * BLOCK, (slots_a + slots_b) * BLOCK
    partner, across = {"rep": 1 - core}, {"width": 1 - wide}

    def local(src, dst, sem):
        return pltpu.make_async_copy(src, dst, sem)

    def remote(src, dst, ssem, rsem, peer):
        return pltpu.make_async_remote_copy(
            src, dst, ssem, rsem, device_id=peer, device_id_type=MESH
        )

    loads = {
        "err": local(err_hbm, err, in_s.at[0]),
        "wd": local(wd_hbm, wd, in_s.at[1]),
        "act": local(act_hbm, nat, in_s.at[2]),
        "hid": local(hid_hbm.at[0], hidb, in_s.at[3]),
    }
    for name in ("err", "wd", "act", "hid"):
        loads[name].start()

    barrier = pltpu.get_barrier_semaphore()
    pl.semaphore_signal(barrier, inc=1, device_id=partner, device_id_type=MESH)
    pl.semaphore_signal(barrier, inc=1, device_id=across, device_id_type=MESH)
    for k in range(1, n):
        peer = {"hidden": lax.rem(z + k, n)}
        pl.semaphore_signal(barrier, inc=1, device_id=peer, device_id_type=MESH)
    pl.semaphore_wait(barrier, n + 1)

    def fill(side, p):
        lanes = pl.ds(p * 128, 128)
        rhs = jnp.concatenate([err[side, lanes, :], err[2 + side, lanes, :]], axis=0)
        tile = units // 3

        def piece(i, carry):
            at = pl.ds(pl.multiple_of(i * tile, 128), tile)
            back = nt(wd[at, :], rhs)
            bt[0, at, :] = back[:, 0:128]
            bt[1, at, :] = back[:, 128:256]
            return carry

        lax.fori_loop(0, 3, piece, 0)

    def per_slot(first, count, action):
        def two(i, carry):
            for k in range(2):
                s = first + 2 * i + k
                base = pl.multiple_of((first + 2 * i) * BLOCK, 8) + k * BLOCK
                action(s, pl.ds(start_ref[s], BLOCK), pl.ds(base, BLOCK))
            return carry

        lax.fori_loop(0, count // 2, two, 0)

    def pick(target):
        def take_a(s, source, place):
            target[place, :] = bt[0, source, :]

        def take_b(s, source, place):
            target[place, :] = bt[1, source, :]

        per_slot(0, slots_a, take_a)
        per_slot(slots_a, slots_b, take_b)

    strip = BLOCK * 4

    def strips(action):
        def step(i, carry):
            action(pl.ds(pl.multiple_of(i * strip, 16), strip))
            return carry

        lax.fori_loop(0, rows // strip, step, 0)

    def push(p):
        return remote(give.at[p], got.at[p], give_s.at[p], give_r.at[p], partner)

    def cross(p):
        return remote(xs.at[p], xr.at[p], x_s.at[p], x_r.at[p], across)

    loads["err"].wait()
    loads["wd"].wait()
    for p in range(pairs):
        fill(1, p)
        pick(give.at[p])
        push(p).start()
        fill(0, p)
        pick(own.at[p])
        push(p).wait_recv()

        def join(at, p=p):
            total = own[p, at, :] + got[p, at, :]
            own[p, at, :] = total
            xs[p, at, :] = total.astype(jnp.bfloat16)

        strips(join)
        cross(p).start()

    loss_core = remote(sq_ref, sq_core, l_s.at[0], l_r.at[0], partner)
    loss_chip = remote(loss_ref, sq_chip, l_s.at[1], l_r.at[1], across)
    loss_core.start()
    loss_core.wait()
    loss_ref[...] = sq_ref[...] + sq_core[...]
    loss_chip.start()

    def flip(source, target, count):
        def step(j, carry):
            lanes = pl.ds(pl.multiple_of(j * 128, 128), 128)
            value = source(lanes).astype(jnp.float32).T.astype(target.dtype)
            if len(target.shape) == 2:
                target[lanes, :] = value
            else:
                for i in range(target.shape[0]):
                    target[i, lanes, :] = value[:, i * 128 : (i + 1) * 128]
            return carry

        lax.fori_loop(0, count // 128, step, 0)

    loads["act"].wait()
    flip(lambda lanes: nat[:, lanes], act_t, units)
    load_fac = local(fac_hbm, nat, in_s.at[2])
    load_fac.start()
    load_fac.wait()
    flip(lambda lanes: nat[:, lanes], fac_t, units)

    loss_chip.wait()
    sq_all[z] = loss_ref[...] + sq_chip[...]

    def share(k):
        return remote(
            sq_all.at[z], sq_all.at[z], z_s.at[k], z_r.at[z],
            {"hidden": lax.rem(z + k, n)},
        )

    for k in range(1, n):
        share(k).start()

    for p in range(pairs):
        push(p).wait_send()

    def keep(s, value):
        return jnp.where(live_ref[s] > 0, value, jnp.zeros_like(value))

    def hid_out(side, p):
        lanes = pl.ds(side * half + p * 128, 128)
        return (
            local(hout.at[side, p, pl.ds(0, rows_a)], ha_hbm.at[:, lanes], h_s.at[0, side, p]),
            local(
                hout.at[side, p, pl.ds(rows_a, rows - rows_a)], hb_hbm.at[:, lanes],
                h_s.at[1, side, p],
            ),
        )

    for side in range(2):
        if side == 0:
            loads["hid"].wait()
        else:
            load_hid = local(hid_hbm.at[1], hidb, in_s.at[3])
            load_hid.start()
            load_hid.wait()
        flip(lambda lanes: hidb[:, lanes], bt, units)
        for p in range(pairs):
            def copy_rows(s, source, place, p=p):
                give[p, place, :] = keep(s, bt[p, source, :])

            per_slot(0, slots_a + slots_b, copy_rows)

            def narrow(at, p=p, side=side):
                hout[side, p, at, :] = give[p, at, :].astype(jnp.bfloat16)

            strips(narrow)
            for copy in hid_out(side, p):
                copy.start()

    def delta_out(p, kind):
        near = pl.ds(p * 128, 128)
        far = pl.ds(half + p * 128, 128)
        pieces = (
            (pl.ds(0, rows_a), (dga_hbm, dua_hbm)[kind]),
            (pl.ds(rows_a, rows - rows_a), (dgb_hbm, dub_hbm)[kind]),
        )
        copies = []
        for i, (part, target) in enumerate(pieces):
            source = outs.at[p, kind, part]
            copies.append(local(source, target.at[:, near], own_s.at[p, kind, i]))
            copies.append(
                remote(
                    source, target.at[:, far], far_s.at[p, kind, i], far_r.at[p, kind, i], partner
                )
            )
        return copies

    for p in range(pairs):
        cross(p).wait_recv()

        def combine(at, p=p):
            own[p, at, :] = own[p, at, :] + xr[p, at, :].astype(jnp.float32)

        strips(combine)

        def scale(s, source, place, p=p):
            total = keep(s, own[p, place, :])
            got[0, place, :] = total * fac_t[p, source, :]
            got[1, place, :] = total * act_t[p, source, :]

        per_slot(0, slots_a + slots_b, scale)
        for kind in range(2):
            def narrow(at, p=p, kind=kind):
                outs[p, kind, at, :] = got[kind, at, :].astype(jnp.bfloat16)

            strips(narrow)
            for copy in delta_out(p, kind):
                copy.start()

    total = None
    for i in range(n):
        @pl.when(z != i)
        def _(i=i):
            remote(
                sq_all.at[i], sq_all.at[i], z_s.at[0], z_r.at[i], partner
            ).wait_recv()

    for i in range(n):
        total = sq_all[i] if total is None else total + sq_all[i]
    loss_ref[...] = total

    for k in range(1, n):
        share(k).wait_send()
    for p in range(pairs):
        cross(p).wait_send()
        for kind in range(2):
            for copy in delta_out(p, kind):
                copy.wait()
        for side in range(2):
            for copy in hid_out(side, p):
                copy.wait()


def backward_call(starts, lives, slots, err, w_down, act, fac, hid, squares):
    (half, units), depth = act.shape, w_down.shape[1]
    rows_a, rows_b = slots[0] * BLOCK, slots[1] * BLOCK
    rows, pairs, n = rows_a + rows_b, half // 128, lax.axis_size("hidden")
    bf, f32 = jnp.bfloat16, jnp.float32
    anywhere = pl.BlockSpec(memory_space=pl.ANY)
    vmem = pl.BlockSpec(memory_space=pltpu.VMEM)
    smem = pl.BlockSpec(memory_space=pltpu.SMEM)
    dma = pltpu.SemaphoreType.DMA
    shape = jax.ShapeDtypeStruct
    return pl.pallas_call(
        functools.partial(backward_kernel, slots),
        out_shape=(
            (shape((rows_a, 2 * half), bf),) * 3
            + (shape((rows_b, 2 * half), bf),) * 3
            + (shape((2, 8, 128), f32),)
        ),
        in_specs=[smem] * 2 + [anywhere] * 5 + [vmem],
        out_specs=(anywhere,) * 6 + (vmem,),
        scratch_shapes=[
            pltpu.VMEM((units, depth), bf),
            pltpu.VMEM((4, half, depth), bf),
            pltpu.VMEM((2, units, 128), f32),
            pltpu.VMEM((pairs, rows, 128), f32),
            pltpu.VMEM((pairs, rows, 128), f32),
            pltpu.VMEM((pairs, rows, 128), f32),
            pltpu.VMEM((pairs, rows, 128), bf),
            pltpu.VMEM((pairs, rows, 128), bf),
            pltpu.VMEM((half, units), f32),
            pltpu.VMEM((pairs, units, 128), f32),
            pltpu.VMEM((pairs, units, 128), f32),
            pltpu.VMEM((half, units), bf),
            pltpu.VMEM((pairs, 2, rows, 128), bf),
            pltpu.VMEM((2, pairs, rows, 128), bf),
            pltpu.VMEM((2, 8, 128), f32),
            pltpu.VMEM((2, 8, 128), f32),
            pltpu.VMEM((n, 2, 8, 128), f32),
            dma((4,)), dma((pairs,)), dma((pairs,)), dma((pairs,)), dma((pairs,)),
            dma((pairs, 2, 2)), dma((pairs, 2, 2)), dma((pairs, 2, 2)), dma((2, 2, pairs)),
            dma((2,)), dma((2,)), dma((n,)), dma((n,)),
        ],
        compiler_params=pltpu.CompilerParams(
            collective_id=1, has_side_effects=True, vmem_limit_bytes=VMEM_LIMIT
        ),
    )(starts, lives, err, w_down, act, fac, hid, squares)


def gradient_kernel(
    dga, dua, ha, dgb, dub, hb, tok, err,
    gga, gua, gda, ggb, gub, gdb,
    left_a, left_b, right, buffer, in_s, out_s,
):
    pieces = 3
    phases = (
        (dga, left_a.at[0], 0, gga), (dua, left_a.at[1], 0, gua), (ha, left_a.at[2], 1, gda),
        (dgb, left_b.at[0], 0, ggb), (dub, left_b.at[1], 0, gub), (hb, left_b.at[2], 2, gdb),
    )
    sources = [(tok, right.at[0])] + [phase[:2] for phase in phases]
    sources.insert(3, (err.at[0], right.at[1]))
    sources.append((err.at[1], right.at[2]))
    loads = [
        pltpu.make_async_copy(src, dst, in_s.at[i]) for i, (src, dst) in enumerate(sources)
    ]
    for load in loads:
        load.start()
    needs = ((0, 1), (2,), (3, 4), (5,), (6,), (7, 8))

    def phase(left, side, out):
        rows = left.shape[0] // pieces

        def copy(i):
            slot = lax.rem(i, 2)
            at = pl.ds(pl.multiple_of(i * rows, 16), rows)
            return pltpu.make_async_copy(
                buffer.at[slot, pl.ds(0, rows)], out.at[at], out_s.at[slot]
            )

        def step(i, carry):
            @pl.when(i >= 2)
            def _():
                copy(i).wait()

            at = pl.ds(pl.multiple_of(i * rows, 16), rows)
            buffer[lax.rem(i, 2), pl.ds(0, rows), :] = nn(left[at, :], right[side]).astype(
                jnp.bfloat16
            )
            copy(i).start()
            return carry

        lax.fori_loop(0, pieces, step, 0)
        for i in (pieces - 2, pieces - 1):
            copy(i).wait()

    for (_, left, side, out), which in zip(phases, needs):
        for i in which:
            loads[i].wait()
        phase(left, side, out)


def gradient_call(dga, dua, ha, dgb, dub, hb, tok, err):
    tokens, depth = tok.shape
    rows_a, rows_b = dga.shape[0], dgb.shape[0]
    bf = jnp.bfloat16
    anywhere = pl.BlockSpec(memory_space=pl.ANY)
    dma = pltpu.SemaphoreType.DMA
    flops = 6 * depth * tokens * (rows_a + rows_b)
    gga, gua, gda, ggb, gub, gdb = pl.pallas_call(
        gradient_kernel,
        out_shape=tuple(
            jax.ShapeDtypeStruct((rows, depth), bf) for rows in (rows_a,) * 3 + (rows_b,) * 3
        ),
        in_specs=[anywhere] * 8,
        out_specs=(anywhere,) * 6,
        scratch_shapes=[
            pltpu.VMEM((3, rows_a, tokens), bf),
            pltpu.VMEM((3, rows_b, tokens), bf),
            pltpu.VMEM((3, tokens, depth), bf),
            pltpu.VMEM((2, rows_a // 3, depth), bf),
            dma((9,)), dma((2,)),
        ],
        compiler_params=pltpu.CompilerParams(vmem_limit_bytes=VMEM_LIMIT),
        cost_estimate=pl.CostEstimate(
            flops=flops, bytes_accessed=4 * depth * (rows_a + rows_b) * 2, transcendentals=0
        ),
    )(dga, dua, ha, dgb, dub, hb, tok, err)
    return gga.T, gua.T, gda, ggb.T, gub.T, gdb


def per_device_fast(tokens, w_gate, w_up, w_down, keep_a, keep_b):
    shard_blocks = keep_a.shape[0]
    slots = (3 * shard_blocks // 4, shard_blocks // 2)
    plans = [block_slots(keep, count) for keep, count in zip((keep_a, keep_b), slots)]
    starts = jnp.concatenate([plan[0] * BLOCK for plan in plans])
    lives = jnp.concatenate([plan[1] for plan in plans])
    masks = jnp.stack([jnp.repeat(keep, BLOCK) for keep in (keep_a, keep_b)])
    masks = masks.astype(jnp.float32) - 1.0
    err, hid, act, fac, tok, squares = forward_call(tokens, w_gate, w_up, w_down, masks)
    *deltas, sums = backward_call(
        starts, lives, slots, err, w_down, act, fac, hid, squares
    )
    token_count = 2 * tokens.shape[0]
    grads = gradient_call(
        *deltas, tok.reshape(token_count, -1), err.reshape(2, token_count, -1)
    )
    copies = lax.axis_size("hidden")
    losses = jnp.sum(sums, axis=(1, 2)) / (copies * token_count * D)
    return (*grads, losses)


def solution(mesh):
    in_specs = (
        P(("groups", "rep"), "width"),
        P(("width", "rep"), "hidden"),
        P(("width", "rep"), "hidden"),
        P("hidden", ("width", "rep")),
        P("hidden"),
        P("hidden"),
    )
    out_specs = (
        P(("width", "rep"), ("groups", "hidden")),
        P(("width", "rep"), ("groups", "hidden")),
        P(("groups", "hidden"), ("width", "rep")),
        P(("width", "rep"), ("groups", "hidden")),
        P(("width", "rep"), ("groups", "hidden")),
        P(("groups", "hidden"), ("width", "rep")),
        P("groups"),
    )
    sizes = mesh.shape
    body = per_device
    if sizes["width"] == 2 and sizes["rep"] == 2 and 2 <= sizes["hidden"] <= 4:
        body = per_device_fast
    return jax.shard_map(
        body, mesh=mesh, in_specs=in_specs, out_specs=out_specs, check_vma=False
    )
```

```python
import functools

import jax
import jax.numpy as jnp
from jax import lax
from jax.experimental import pallas as pl
from jax.experimental.pallas import tpu as pltpu
from jax.sharding import PartitionSpec as P


D = 5120
BLOCK = 108


def block_slots(keep_mask, slot_count):
    positions = jnp.arange(keep_mask.shape[0], dtype=jnp.int32)
    ranking = jnp.cumsum(keep_mask) - 1
    slot_ids = jnp.arange(slot_count, dtype=jnp.int32)
    matches = keep_mask[None, :] * (ranking[None, :] == slot_ids[:, None]).astype(jnp.int32)
    block_index = jnp.sum(matches * positions[None, :], axis=1)
    block_live = jnp.sum(matches, axis=1)
    return (block_index, block_live)


def pick_blocks(matrix, block_index, block_live, dim_axis):
    if dim_axis == 1:
        grouped = matrix.reshape(matrix.shape[0], -1, BLOCK)
        picked = jnp.take(grouped, block_index, axis=1) * block_live[None, :, None].astype(
            matrix.dtype
        )
        return picked.reshape(matrix.shape[0], -1)
    grouped = matrix.reshape(-1, BLOCK, matrix.shape[1])
    picked = jnp.take(grouped, block_index, axis=0) * block_live[:, None, None].astype(matrix.dtype)
    return picked.reshape(-1, matrix.shape[1])


def per_device(tokens, w_gate, w_up, w_down, keep_a, keep_b):
    gathered = lax.all_to_all(tokens, "rep", split_axis=1, concat_axis=0, tiled=True)
    part_gate = jnp.dot(gathered, w_gate, preferred_element_type=jnp.float32)
    part_up = jnp.dot(gathered, w_up, preferred_element_type=jnp.float32)
    gate_value, up_value = lax.psum((part_gate, part_up), ("width", "rep"))
    sigmoid_term = jax.nn.sigmoid(gate_value)
    activation = gate_value * sigmoid_term
    slope_term = sigmoid_term * (1.0 + gate_value * (1.0 - sigmoid_term))
    hidden = (activation * up_value).astype(jnp.bfloat16)
    shard_blocks = keep_a.shape[0]
    variant_plans = ((keep_a, 3 * shard_blocks // 4), (keep_b, shard_blocks // 2))
    differences = jnp.stack(
        [
            -jnp.dot(
                hidden * (1 - jnp.repeat(keep_mask, BLOCK)).astype(jnp.bfloat16)[None, :],
                w_down,
                preferred_element_type=jnp.float32,
            )
            for keep_mask, slot_count in variant_plans
        ]
    )
    scale_count = gathered.shape[0] * D
    totals = lax.psum(differences, "hidden")
    squares = jnp.sum(totals * totals, axis=(1, 2))
    losses = lax.psum(squares, ("width", "rep")) / scale_count
    errors = totals.astype(jnp.bfloat16)
    slot_plans = [block_slots(keep_mask, slot_count) for keep_mask, slot_count in variant_plans]
    back_terms = [
        jnp.einsum(
            "td,fd->tf",
            errors[variant],
            pick_blocks(w_down, slot_plans[variant][0], slot_plans[variant][1], 0),
            preferred_element_type=jnp.float32,
        )
        for variant in range(2)
    ]
    back_a, back_b = lax.psum((back_terms[0], back_terms[1]), ("width", "rep"))
    results = []
    for variant, back_total in ((0, back_a), (1, back_b)):
        block_index, block_live = slot_plans[variant]
        keep_mask = variant_plans[variant][0]
        up_slot = pick_blocks(up_value, block_index, block_live, 1)
        slope_slot = pick_blocks(slope_term, block_index, block_live, 1)
        act_slot = pick_blocks(activation, block_index, block_live, 1)
        hidden_slot = pick_blocks(hidden, block_index, block_live, 1)
        delta_gate = (back_total * up_slot * slope_slot).astype(jnp.bfloat16)
        delta_up = (back_total * act_slot).astype(jnp.bfloat16)
        grad_gate = jnp.einsum(
            "td,tf->df", gathered, delta_gate, preferred_element_type=jnp.float32
        )
        grad_up = jnp.einsum("td,tf->df", gathered, delta_up, preferred_element_type=jnp.float32)
        grad_down = jnp.einsum(
            "tf,td->fd", hidden_slot, errors[variant], preferred_element_type=jnp.float32
        )
        results.append(
            (
                grad_gate.astype(jnp.bfloat16),
                grad_up.astype(jnp.bfloat16),
                grad_down.astype(jnp.bfloat16),
            )
        )
    return (
        results[0][0],
        results[0][1],
        results[0][2],
        results[1][0],
        results[1][1],
        results[1][2],
        losses,
    )


MESH = pl.DeviceIdType.MESH
VMEM_LIMIT = 63 << 20


def nt(a, b):
    return lax.dot_general(a, b, (((1,), (1,)), ((), ())), preferred_element_type=jnp.float32)


def nn(a, b):
    return jnp.dot(a, b, preferred_element_type=jnp.float32)


def forward_kernel(
    chunks, block, slots,
    tok_hbm, wg_hbm, wu_hbm, wd_hbm, keep_a_ref, keep_b_ref,
    err_hbm, hid_hbm, act_hbm, fac_hbm, tok_out, sq_ref, plan_ref,
    tok, wgb, wub, wd, part, stage, ring, xs, xr, hid, lhs, zp, zs, zr, errs, mask_ref,
    tok_s, tok_r, w_sem, wd_sem, st_s, ring_r, x_s, x_r, hid_s, hid_r, z_s, z_r, keep_s, err_s,
):
    n = lax.axis_size("hidden")
    z, wide, core = lax.axis_index("hidden"), lax.axis_index("width"), lax.axis_index("rep")
    depth, units = wg_hbm.shape
    half = tok_hbm.shape[0]
    blocks = units // block
    partner, across = {"rep": 1 - core}, {"width": 1 - wide}

    def local(src, dst, sem):
        return pltpu.make_async_copy(src, dst, sem)

    def remote(src, dst, ssem, rsem, peer):
        return pltpu.make_async_remote_copy(
            src, dst, ssem, rsem, device_id=peer, device_id_type=MESH
        )

    def weights(j):
        lanes = pl.ds(pl.multiple_of(j * block, 128), block)
        slot = lax.rem(j, 2)
        return (
            local(wg_hbm.at[:, lanes], wgb.at[slot], w_sem.at[0, slot]),
            local(wu_hbm.at[:, lanes], wub.at[slot], w_sem.at[1, slot]),
        )

    for j in range(2):
        for copy in weights(j):
            copy.start()
    mine = local(
        tok_hbm.at[:, pl.ds(pl.multiple_of(core * depth, 128), depth)], tok.at[0], wd_sem
    )
    mine.start()
    load_down = local(wd_hbm, wd, wd_sem)

    barrier = pltpu.get_barrier_semaphore()
    pl.semaphore_signal(barrier, inc=1, device_id=partner, device_id_type=MESH)
    pl.semaphore_signal(barrier, inc=1, device_id=across, device_id_type=MESH)

    @pl.when(z > 0)
    def _():
        pl.semaphore_signal(barrier, inc=1, device_id={"hidden": z - 1}, device_id_type=MESH)

    @pl.when(z < n - 1)
    def _():
        pl.semaphore_signal(barrier, inc=1, device_id={"hidden": z + 1}, device_id_type=MESH)

    @pl.when((z == 0) | (z == n - 1))
    def _():
        pl.semaphore_wait(barrier, 3)

    @pl.when((z > 0) & (z < n - 1))
    def _():
        pl.semaphore_wait(barrier, 4)

    give = remote(
        tok_hbm.at[:, pl.ds(pl.multiple_of((1 - core) * depth, 128), depth)],
        tok.at[1], tok_s, tok_r, partner,
    )
    give.start()
    sq_ref[...] = jnp.zeros_like(sq_ref)
    shard_blocks = keep_a_ref.shape[0]
    keeps = (keep_a_ref, keep_b_ref)
    unit = lax.broadcasted_iota(jnp.int32, (1, units), 1)
    for k, keep in enumerate(keeps):
        level = jnp.zeros((1, units), jnp.float32)
        before = 1
        for b in range(shard_blocks):
            jump = (keep[b] - before).astype(jnp.float32)
            level = level + jnp.where(unit >= b * BLOCK, jump, 0.0)
            before = keep[b]
        mask_ref[k : k + 1, :] = level
    slot = lax.broadcasted_iota(jnp.int32, (1, 128), 1)
    start, live = jnp.zeros((1, 128), jnp.int32), jnp.zeros((1, 128), jnp.int32)
    base = 0
    for keep, count in zip(keeps, slots):
        seen = base
        for b in range(shard_blocks):
            hit = jnp.where(slot == seen, keep[b], 0)
            live = live + hit
            start = start + hit * (b * BLOCK)
            seen = seen + keep[b]
        base += count
    plan_ref[0:1, :] = start
    plan_ref[1:2, :] = live
    mine.wait()
    give.wait()
    load_down.start()
    keep_tok = local(tok, tok_out, tok_s)
    keep_tok.start()

    def push(j):
        return remote(
            stage.at[lax.rem(j, 2)], ring.at[lax.rem(j, 4)],
            st_s.at[lax.rem(j, 2)], ring_r.at[lax.rem(j, 4)], partner,
        )

    first = chunks[0][1]

    def cross_block(j):
        lanes = pl.ds(pl.multiple_of(j * block, 128), block)
        return remote(
            xs.at[:, pl.ds(0, first), lanes], xr.at[:, pl.ds(0, first), lanes],
            x_s.at[0], x_r.at[0], across,
        )

    def cross(c):
        rows = pl.ds(*chunks[c])
        return remote(xs.at[:, rows, :], xr.at[:, rows, :], x_s.at[c], x_r.at[c], across)

    def take(j):
        lanes = pl.ds(pl.multiple_of(j * block, 128), block)
        slot = lax.rem(j, 4)
        push(j).wait_recv()
        for i in range(2):
            total = part[i, :, lanes] + ring[slot, i]
            part[i, :, lanes] = total
            xs[i, :, lanes] = total.astype(jnp.bfloat16)
        cross_block(j).start()

    def step(j, carry):
        for copy in weights(j):
            copy.wait()
        slot = lax.rem(j, 2)
        lanes = pl.ds(pl.multiple_of(j * block, 128), block)

        @pl.when(j >= 2)
        def _():
            push(j).wait_send()

        stage[slot, 0] = nn(tok[1], wgb[slot])
        stage[slot, 1] = nn(tok[1], wub[slot])
        push(j).start()

        @pl.when(j >= 1)
        def _():
            take(j - 1)

        part[0, :, lanes] = nn(tok[0], wgb[slot])
        part[1, :, lanes] = nn(tok[0], wub[slot])

        @pl.when(j + 2 < blocks)
        def _():
            for copy in weights(j + 2):
                copy.start()

        return carry

    lax.fori_loop(0, blocks, step, 0)
    take(blocks - 1)
    for c in range(1, len(chunks)):
        cross(c).start()
    for j in (blocks - 2, blocks - 1):
        push(j).wait_send()
    load_down.wait()

    def swap_hidden(c):
        rows = pl.ds(*chunks[c])
        return remote(hid.at[0, rows], hid.at[1, rows], hid_s.at[c], hid_r.at[c], partner)

    def keep_out(c):
        rows = pl.ds(*chunks[c])
        return (
            local(part.at[0, rows], act_hbm.at[rows], keep_s.at[0, c]),
            local(part.at[1, rows], fac_hbm.at[rows], keep_s.at[1, c]),
        )

    def activate(c):
        start, count = chunks[c]
        rows = pl.ds(start, count)
        cross(c).wait_recv()

        def lane_block(j, carry):
            lanes = pl.ds(pl.multiple_of(j * block, 128), block)
            gate = part[0, rows, lanes] + xr[0, rows, lanes].astype(jnp.float32)
            up = part[1, rows, lanes] + xr[1, rows, lanes].astype(jnp.float32)
            sigmoid = jax.nn.sigmoid(gate)
            act = gate * sigmoid
            hid[0, rows, lanes] = (act * up).astype(jnp.bfloat16)
            part[0, rows, lanes] = act
            part[1, rows, lanes] = up * (sigmoid * (1.0 + gate * (1.0 - sigmoid)))
            return carry

        lax.fori_loop(0, blocks, lane_block, 0)
        swap_hidden(c).start()
        for copy in keep_out(c):
            copy.start()

    def differ(c):
        start, count = chunks[c]
        rows = pl.ds(start, count)
        swap_hidden(c).wait_recv()

        def masked(j, carry):
            lanes = pl.ds(pl.multiple_of(j * block, 128), block)
            for side in range(2):
                value = hid[side, rows, lanes]
                for k in range(2):
                    drop = mask_ref[k : k + 1, lanes].astype(jnp.bfloat16)
                    lhs[pl.ds((2 * k + side) * count, count), lanes] = value * drop
            return carry

        lax.fori_loop(0, blocks, masked, 0)

        def columns(j, carry):
            lanes = pl.ds(pl.multiple_of(j * 256, 128), 256)
            zp[pl.ds(4 * start, 4 * count), lanes] = nn(lhs[pl.ds(0, 4 * count), :], wd[:, lanes])
            return carry

        lax.fori_loop(0, depth // 256, columns, 0)

    def z_copy(c, d, q):
        start, count = chunks[c]
        rows = pl.ds(pl.multiple_of(4 * start + q * count, 16), count)
        peer = {"hidden": z + 1 - 2 * d}
        return remote(zs.at[d, rows], zr.at[d, rows], z_s.at[c, d, q], z_r.at[c, d, q], peer)

    def has_up(d):
        return ((d == 0) & (z > 0)) | ((d == 1) & (z < n - 1))

    def has_down(d):
        return ((d == 0) & (z < n - 1)) | ((d == 1) & (z > 0))

    def hop(c, d, q):
        start, count = chunks[c]
        rows = pl.ds(pl.multiple_of(4 * start + q * count, 16), count)

        @pl.when(has_up(d))
        def _():
            z_copy(c, d, q).wait_recv()

        @pl.when(has_up(d) & has_down(d))
        def _():
            total = zp[rows, :] + zr[d, rows, :].astype(jnp.float32)
            zs[d, rows, :] = total.astype(jnp.bfloat16)

        @pl.when(has_down(d) & jnp.logical_not(has_up(d)))
        def _():
            zs[d, rows, :] = zp[rows, :].astype(jnp.bfloat16)

        @pl.when(has_down(d))
        def _():
            z_copy(c, d, q).start()

    def err_out(c, q):
        start, count = chunks[c]
        rows = pl.ds(pl.multiple_of(4 * start + q * count, 16), count)
        return local(errs.at[rows], err_hbm.at[q, pl.ds(start, count)], err_s.at[c, q])

    def finish(c, q):
        start, count = chunks[c]
        rows = pl.ds(pl.multiple_of(4 * start + q * count, 16), count)

        def settle(total):
            errs[rows, :] = total.astype(jnp.bfloat16)
            square = total * total
            folded = square[0:8]
            for i in range(8, count, 8):
                folded = folded + square[i : i + 8]
            narrow = folded[:, 0:128]
            for i in range(128, depth, 128):
                narrow = narrow + folded[:, i : i + 128]
            k = q // 2
            sq_ref[k] = sq_ref[k] + narrow

        @pl.when(z == 0)
        def _():
            settle(zp[rows, :] + zr[1, rows, :].astype(jnp.float32))

        @pl.when(z == n - 1)
        def _():
            settle(zp[rows, :] + zr[0, rows, :].astype(jnp.float32))

        @pl.when((z > 0) & (z < n - 1))
        def _():
            settle(
                zp[rows, :]
                + (zr[0, rows, :].astype(jnp.float32) + zr[1, rows, :].astype(jnp.float32))
            )

        err_out(c, q).start()

    early = (2 * z) // n
    late = 1 - early
    edge = (z == 0) | (z == n - 1)
    last = len(chunks) - 1

    def each(*actions):
        def piece(q, carry):
            for action, c, args in actions:
                action(c, *args, q)
            return carry

        lax.fori_loop(0, 4, piece, 0)

    for c in range(len(chunks)):
        activate(c)
        differ(c)

        @pl.when(edge)
        def _(c=c):
            each((hop, c, (early,)))
            if c > 1:
                each((hop, c - 2, (late,)), (finish, c - 2, ()))

        @pl.when(jnp.logical_not(edge))
        def _(c=c):
            behind = ((hop, c - 1, (late,)), (finish, c - 1, ())) if c > 0 else ()
            each(*behind, (hop, c, (early,)))

    @pl.when(edge)
    def _():
        each((hop, last - 1, (late,)), (finish, last - 1, ()))

    each((hop, last, (late,)), (finish, last, ()))

    keep_tok.wait()
    for side in range(2):
        local(hid.at[side], hid_hbm.at[side], w_sem.at[0, side]).start()
    for side in range(2):
        local(hid.at[side], hid_hbm.at[side], w_sem.at[0, side]).wait()
    for c in range(len(chunks)):
        cross(c).wait_send()
        swap_hidden(c).wait_send()
        for copy in keep_out(c):
            copy.wait()

        def drain(q, carry, c=c):
            err_out(c, q).wait()
            for d in range(2):
                @pl.when(has_down(d))
                def _():
                    z_copy(c, d, q).wait_send()
            return carry

        lax.fori_loop(0, 4, drain, 0)


def forward_call(slots, tokens, w_gate, w_up, w_down, keep_a, keep_b):
    half, (depth, units) = tokens.shape[0], w_gate.shape
    block = 384 if units % 384 == 0 else 128
    counts = [half * part // 16 for part in (4, 3, 3, 2, 2, 2)]
    chunks = tuple((sum(counts[:i]), count) for i, count in enumerate(counts))
    parts = len(chunks)
    bf, f32 = jnp.bfloat16, jnp.float32
    anywhere = pl.BlockSpec(memory_space=pl.ANY)
    vmem = pl.BlockSpec(memory_space=pltpu.VMEM)
    smem = pl.BlockSpec(memory_space=pltpu.SMEM)
    dma = pltpu.SemaphoreType.DMA
    return pl.pallas_call(
        functools.partial(forward_kernel, chunks, block, slots),
        out_shape=(
            jax.ShapeDtypeStruct((4, half, depth), bf),
            jax.ShapeDtypeStruct((2, half, units), bf),
            jax.ShapeDtypeStruct((half, units), f32),
            jax.ShapeDtypeStruct((half, units), f32),
            jax.ShapeDtypeStruct((2, half, depth), bf),
            jax.ShapeDtypeStruct((2, 8, 128), f32),
            jax.ShapeDtypeStruct((2, 128), jnp.int32),
        ),
        in_specs=[anywhere] * 4 + [smem] * 2,
        out_specs=(anywhere,) * 5 + (vmem,) * 2,
        scratch_shapes=[
            pltpu.VMEM((2, half, depth), bf),
            pltpu.VMEM((2, depth, block), bf),
            pltpu.VMEM((2, depth, block), bf),
            pltpu.VMEM((units, depth), bf),
            pltpu.VMEM((2, half, units), f32),
            pltpu.VMEM((2, 2, half, block), f32),
            pltpu.VMEM((4, 2, half, block), f32),
            pltpu.VMEM((2, half, units), bf),
            pltpu.VMEM((2, half, units), bf),
            pltpu.VMEM((2, half, units), bf),
            pltpu.VMEM((4 * max(counts), units), bf),
            pltpu.VMEM((4 * half, depth), f32),
            pltpu.VMEM((2, 4 * half, depth), bf),
            pltpu.VMEM((2, 4 * half, depth), bf),
            pltpu.VMEM((4 * half, depth), bf),
            pltpu.VMEM((2, units), f32),
            dma, dma, dma((2, 2)), dma, dma((2,)), dma((4,)),
            dma((parts,)), dma((parts,)), dma((parts,)), dma((parts,)),
            dma((parts, 2, 4)), dma((parts, 2, 4)), dma((2, parts)), dma((parts, 4)),
        ],
        compiler_params=pltpu.CompilerParams(
            collective_id=0, has_side_effects=True, vmem_limit_bytes=VMEM_LIMIT
        ),
    )(tokens, w_gate, w_up, w_down, keep_a, keep_b)


def backward_kernel(
    slots,
    plan_ref, err_hbm, wd_hbm, act_hbm, fac_hbm, hid_hbm, sq_ref,
    dga_hbm, dua_hbm, ha_hbm, dgb_hbm, dub_hbm, hb_hbm, loss_ref,
    wd, err, bt, give, got, own, xs, xr, nat, act_t, fac_t, hidb, outs, hout,
    sq_core, sq_chip, sq_all,
    in_s, give_s, give_r, x_s, x_r, own_s, far_s, far_r, h_s, l_s, l_r, z_s, z_r,
):
    n = lax.axis_size("hidden")
    z, wide, core = lax.axis_index("hidden"), lax.axis_index("width"), lax.axis_index("rep")
    units, depth = wd_hbm.shape
    half = act_hbm.shape[0]
    pairs = half // 128
    slots_a, slots_b = slots
    rows_a, rows = slots_a * BLOCK, (slots_a + slots_b) * BLOCK
    partner, across = {"rep": 1 - core}, {"width": 1 - wide}

    def local(src, dst, sem):
        return pltpu.make_async_copy(src, dst, sem)

    def remote(src, dst, ssem, rsem, peer):
        return pltpu.make_async_remote_copy(
            src, dst, ssem, rsem, device_id=peer, device_id_type=MESH
        )

    load_err = local(err_hbm, err, in_s.at[0])
    load_act = local(act_hbm, nat, in_s.at[1])
    load_hid = local(hid_hbm.at[0], hidb, in_s.at[2])
    tile = units // 3

    def load_down(i):
        at = pl.ds(pl.multiple_of(i * tile, 128), tile)
        return local(wd_hbm.at[at], wd.at[at], in_s.at[3 + i])

    load_err.start()
    for i in range(3):
        load_down(i).start()

    barrier = pltpu.get_barrier_semaphore()
    pl.semaphore_signal(barrier, inc=1, device_id=partner, device_id_type=MESH)
    pl.semaphore_signal(barrier, inc=1, device_id=across, device_id_type=MESH)
    for k in range(1, n):
        peer = {"hidden": lax.rem(z + k, n)}
        pl.semaphore_signal(barrier, inc=1, device_id=peer, device_id_type=MESH)
    pl.semaphore_wait(barrier, n + 1)
    loss_core = remote(sq_ref, sq_core, l_s.at[0], l_r.at[0], partner)
    loss_chip = remote(loss_ref, sq_chip, l_s.at[1], l_r.at[1], across)
    loss_core.start()

    def fill(side, p):
        lanes = pl.ds(p * 128, 128)
        rhs = jnp.concatenate([err[side, lanes, :], err[2 + side, lanes, :]], axis=0)

        def piece(i, carry):
            if side == 1 and p == 0:
                load_down(i).wait()
            at = pl.ds(pl.multiple_of(i * tile, 128), tile)
            back = nt(wd[at, :], rhs)
            bt[0, at, :] = back[:, 0:128]
            bt[1, at, :] = back[:, 128:256]
            return carry

        lax.fori_loop(0, 3, piece, 0)

    def per_slot(first, count, action):
        def two(i, carry):
            for k in range(2):
                s = first + 2 * i + k
                base = pl.multiple_of((first + 2 * i) * BLOCK, 8) + k * BLOCK
                action(s, pl.ds(plan_ref[0, s], BLOCK), pl.ds(base, BLOCK))
            return carry

        lax.fori_loop(0, count // 2, two, 0)

    counts = ((0, slots_a), (slots_a, slots_b))
    spans = (pl.ds(0, rows_a), pl.ds(rows_a, rows - rows_a))

    def pick(target, v):
        def take(s, source, place):
            target[place, :] = bt[v, source, :]

        per_slot(*counts[v], take)

    strip = BLOCK * 4

    def strips(v, action):
        base = (0, rows_a)[v]

        def step(i, carry):
            action(pl.ds(pl.multiple_of(base + i * strip, 16), strip))
            return carry

        lax.fori_loop(0, (rows_a, rows - rows_a)[v] // strip, step, 0)

    def push(p, v):
        return remote(
            give.at[p, spans[v]], got.at[p, spans[v]], give_s.at[p, v], give_r.at[p, v], partner
        )

    def cross(p, v):
        return remote(xs.at[p, spans[v]], xr.at[p, spans[v]], x_s.at[p, v], x_r.at[p, v], across)

    load_err.wait()
    for p in range(pairs):
        fill(1, p)
        for v in range(2):
            pick(give.at[p], v)
            push(p, v).start()
        if p == 0:
            load_act.start()
            load_hid.start()
            loss_core.wait()
            loss_ref[...] = sq_ref[...] + sq_core[...]
            loss_chip.start()
        fill(0, p)
        for v in range(2):
            pick(own.at[p], v)
            push(p, v).wait_recv()

            def join(at, p=p):
                total = own[p, at, :] + got[p, at, :]
                own[p, at, :] = total
                xs[p, at, :] = total.astype(jnp.bfloat16)

            strips(v, join)
            cross(p, v).start()

    def flip(source, target, count):
        def step(j, carry):
            lanes = pl.ds(pl.multiple_of(j * 128, 128), 128)
            value = source(lanes).astype(jnp.float32).T.astype(target.dtype)
            if len(target.shape) == 2:
                target[lanes, :] = value
            else:
                for i in range(target.shape[0]):
                    target[i, lanes, :] = value[:, i * 128 : (i + 1) * 128]
            return carry

        lax.fori_loop(0, count // 128, step, 0)

    load_act.wait()
    flip(lambda lanes: nat[:, lanes], act_t, units)
    load_fac = local(fac_hbm, nat, in_s.at[1])
    load_fac.start()
    load_fac.wait()
    flip(lambda lanes: nat[:, lanes], fac_t, units)

    loss_chip.wait()
    sq_all[z] = loss_ref[...] + sq_chip[...]

    def share(k):
        return remote(
            sq_all.at[z], sq_all.at[z], z_s.at[k], z_r.at[z],
            {"hidden": lax.rem(z + k, n)},
        )

    for k in range(1, n):
        share(k).start()

    for p in range(pairs):
        for v in range(2):
            push(p, v).wait_send()

    def keep(s, value):
        return jnp.where(plan_ref[1, s] > 0, value, jnp.zeros_like(value))

    def hid_out(side, p):
        lanes = pl.ds(side * half + p * 128, 128)
        return (
            local(hout.at[side, p, pl.ds(0, rows_a)], ha_hbm.at[:, lanes], h_s.at[0, side, p]),
            local(
                hout.at[side, p, pl.ds(rows_a, rows - rows_a)], hb_hbm.at[:, lanes],
                h_s.at[1, side, p],
            ),
        )

    for side in range(2):
        if side == 0:
            load_hid.wait()
        else:
            next_hid = local(hid_hbm.at[1], hidb, in_s.at[2])
            next_hid.start()
            next_hid.wait()
        flip(lambda lanes: hidb[:, lanes], bt, units)
        for p in range(pairs):
            def copy_rows(s, source, place, p=p):
                give[p, place, :] = keep(s, bt[p, source, :])

            per_slot(0, slots_a + slots_b, copy_rows)

            def narrow(at, p=p, side=side):
                hout[side, p, at, :] = give[p, at, :].astype(jnp.bfloat16)

            for v in range(2):
                strips(v, narrow)
            for copy in hid_out(side, p):
                copy.start()

    def delta_out(p, kind, v):
        near = pl.ds(p * 128, 128)
        far = pl.ds(half + p * 128, 128)
        source = outs.at[p, kind, spans[v]]
        target = ((dga_hbm, dgb_hbm), (dua_hbm, dub_hbm))[kind][v]
        return (
            remote(
                source, target.at[:, far], far_s.at[p, kind, v], far_r.at[p, kind, v], partner
            ),
            local(source, target.at[:, near], own_s.at[p, kind, v]),
        )

    for p in range(pairs):
        for v in range(2):
            cross(p, v).wait_recv()

            def combine(at, p=p):
                own[p, at, :] = own[p, at, :] + xr[p, at, :].astype(jnp.float32)

            strips(v, combine)

            def scale(s, source, place, p=p):
                total = keep(s, own[p, place, :])
                got[0, place, :] = total * fac_t[p, source, :]
                got[1, place, :] = total * act_t[p, source, :]

            per_slot(*counts[v], scale)
            for kind in range(2):
                def narrow(at, p=p, kind=kind):
                    outs[p, kind, at, :] = got[kind, at, :].astype(jnp.bfloat16)

                strips(v, narrow)
                for copy in delta_out(p, kind, v):
                    copy.start()

    total = None
    for i in range(n):
        @pl.when(z != i)
        def _(i=i):
            remote(
                sq_all.at[i], sq_all.at[i], z_s.at[0], z_r.at[i], partner
            ).wait_recv()

    for i in range(n):
        total = sq_all[i] if total is None else total + sq_all[i]
    loss_ref[...] = total

    for k in range(1, n):
        share(k).wait_send()
    for p in range(pairs):
        for v in range(2):
            cross(p, v).wait_send()
            for kind in range(2):
                for copy in delta_out(p, kind, v):
                    copy.wait()
        for side in range(2):
            for copy in hid_out(side, p):
                copy.wait()


def backward_call(plan, slots, err, w_down, act, fac, hid, squares):
    (half, units), depth = act.shape, w_down.shape[1]
    rows_a, rows_b = slots[0] * BLOCK, slots[1] * BLOCK
    rows, pairs, n = rows_a + rows_b, half // 128, lax.axis_size("hidden")
    bf, f32 = jnp.bfloat16, jnp.float32
    anywhere = pl.BlockSpec(memory_space=pl.ANY)
    vmem = pl.BlockSpec(memory_space=pltpu.VMEM)
    smem = pl.BlockSpec(memory_space=pltpu.SMEM)
    dma = pltpu.SemaphoreType.DMA
    shape = jax.ShapeDtypeStruct
    return pl.pallas_call(
        functools.partial(backward_kernel, slots),
        out_shape=(
            (shape((rows_a, 2 * half), bf),) * 3
            + (shape((rows_b, 2 * half), bf),) * 3
            + (shape((2, 8, 128), f32),)
        ),
        in_specs=[smem] + [anywhere] * 5 + [vmem],
        out_specs=(anywhere,) * 6 + (vmem,),
        scratch_shapes=[
            pltpu.VMEM((units, depth), bf),
            pltpu.VMEM((4, half, depth), bf),
            pltpu.VMEM((2, units, 128), f32),
            pltpu.VMEM((pairs, rows, 128), f32),
            pltpu.VMEM((pairs, rows, 128), f32),
            pltpu.VMEM((pairs, rows, 128), f32),
            pltpu.VMEM((pairs, rows, 128), bf),
            pltpu.VMEM((pairs, rows, 128), bf),
            pltpu.VMEM((half, units), f32),
            pltpu.VMEM((pairs, units, 128), f32),
            pltpu.VMEM((pairs, units, 128), f32),
            pltpu.VMEM((half, units), bf),
            pltpu.VMEM((pairs, 2, rows, 128), bf),
            pltpu.VMEM((2, pairs, rows, 128), bf),
            pltpu.VMEM((2, 8, 128), f32),
            pltpu.VMEM((2, 8, 128), f32),
            pltpu.VMEM((n, 2, 8, 128), f32),
            dma((6,)), dma((pairs, 2)), dma((pairs, 2)), dma((pairs, 2)), dma((pairs, 2)),
            dma((pairs, 2, 2)), dma((pairs, 2, 2)), dma((pairs, 2, 2)), dma((2, 2, pairs)),
            dma((2,)), dma((2,)), dma((n,)), dma((n,)),
        ],
        compiler_params=pltpu.CompilerParams(
            collective_id=1, has_side_effects=True, vmem_limit_bytes=VMEM_LIMIT
        ),
    )(plan, err, w_down, act, fac, hid, squares)


def gradient_kernel(
    scale,
    dga, dua, ha, dgb, dub, hb, tok, err, sums_ref,
    gga, gua, gda, ggb, gub, gdb, loss_ref,
    left_a, left_b, right, buffer, in_s, out_s,
):
    pieces = 2
    phases = (
        (dga, left_a.at[0], 0, gga), (dua, left_a.at[1], 0, gua), (ha, left_a.at[2], 1, gda),
        (dgb, left_b.at[0], 0, ggb), (dub, left_b.at[1], 0, gub), (hb, left_b.at[2], 2, gdb),
    )
    sources = [(tok, right.at[0])] + [phase[:2] for phase in phases]
    sources.insert(3, (err.at[0], right.at[1]))
    sources.append((err.at[1], right.at[2]))
    loads = [
        pltpu.make_async_copy(src, dst, in_s.at[i]) for i, (src, dst) in enumerate(sources)
    ]
    for load in loads:
        load.start()
    needs = ((0, 1), (2,), (3, 4), (5,), (6,), (7, 8))

    for k in range(2):
        loss_ref[k] = jnp.sum(sums_ref[k]) * scale
    pending = []
    for (_, left, side, out), which in zip(phases, needs):
        for i in which:
            loads[i].wait()
        rows = left.shape[0] // pieces
        for i in range(pieces):
            slot = len(pending) % 2
            if len(pending) > 1:
                pending[-2].wait()
            at = pl.ds(i * rows, rows)
            buffer[slot, pl.ds(0, rows), :] = nn(left[at, :], right[side]).astype(jnp.bfloat16)
            copy = pltpu.make_async_copy(
                buffer.at[slot, pl.ds(0, rows)], out.at[at], out_s.at[slot]
            )
            copy.start()
            pending.append(copy)
    for copy in pending[-2:]:
        copy.wait()


def gradient_call(scale, dga, dua, ha, dgb, dub, hb, tok, err, sums):
    tokens, depth = tok.shape
    rows_a, rows_b = dga.shape[0], dgb.shape[0]
    bf = jnp.bfloat16
    anywhere = pl.BlockSpec(memory_space=pl.ANY)
    dma = pltpu.SemaphoreType.DMA
    flops = 6 * depth * tokens * (rows_a + rows_b)
    gga, gua, gda, ggb, gub, gdb, losses = pl.pallas_call(
        functools.partial(gradient_kernel, scale),
        out_shape=tuple(
            jax.ShapeDtypeStruct((rows, depth), bf) for rows in (rows_a,) * 3 + (rows_b,) * 3
        ) + (jax.ShapeDtypeStruct((2,), jnp.float32),),
        in_specs=[anywhere] * 8 + [pl.BlockSpec(memory_space=pltpu.VMEM)],
        out_specs=(anywhere,) * 6 + (pl.BlockSpec(memory_space=pltpu.SMEM),),
        scratch_shapes=[
            pltpu.VMEM((3, rows_a, tokens), bf),
            pltpu.VMEM((3, rows_b, tokens), bf),
            pltpu.VMEM((3, tokens, depth), bf),
            pltpu.VMEM((2, rows_a // 2, depth), bf),
            dma((9,)), dma((2,)),
        ],
        compiler_params=pltpu.CompilerParams(vmem_limit_bytes=VMEM_LIMIT),
        cost_estimate=pl.CostEstimate(
            flops=flops, bytes_accessed=4 * depth * (rows_a + rows_b) * 2, transcendentals=0
        ),
    )(dga, dua, ha, dgb, dub, hb, tok, err, sums)
    return gga.T, gua.T, gda, ggb.T, gub.T, gdb, losses


def per_device_fast(tokens, w_gate, w_up, w_down, keep_a, keep_b):
    shard_blocks = keep_a.shape[0]
    slots = (3 * shard_blocks // 4, shard_blocks // 2)
    err, hid, act, fac, tok, squares, plan = forward_call(
        slots, tokens, w_gate, w_up, w_down, keep_a, keep_b
    )
    *deltas, sums = backward_call(plan, slots, err, w_down, act, fac, hid, squares)
    token_count = 2 * tokens.shape[0]
    scale = 1.0 / (lax.axis_size("hidden") * token_count * D)
    return gradient_call(
        scale, *deltas, tok.reshape(token_count, -1), err.reshape(2, token_count, -1), sums
    )


def solution(mesh):
    in_specs = (
        P(("groups", "rep"), "width"),
        P(("width", "rep"), "hidden"),
        P(("width", "rep"), "hidden"),
        P("hidden", ("width", "rep")),
        P("hidden"),
        P("hidden"),
    )
    out_specs = (
        P(("width", "rep"), ("groups", "hidden")),
        P(("width", "rep"), ("groups", "hidden")),
        P(("groups", "hidden"), ("width", "rep")),
        P(("width", "rep"), ("groups", "hidden")),
        P(("width", "rep"), ("groups", "hidden")),
        P(("groups", "hidden"), ("width", "rep")),
        P("groups"),
    )
    sizes = mesh.shape
    body = per_device
    if sizes["width"] == 2 and sizes["rep"] == 2 and 2 <= sizes["hidden"] <= 4:
        body = per_device_fast
    return jax.shard_map(
        body, mesh=mesh, in_specs=in_specs, out_specs=out_specs, check_vma=False
    )
```

```python
import functools

import jax
import jax.numpy as jnp
from jax import lax
from jax.experimental import pallas as pl
from jax.experimental.pallas import tpu as pltpu
from jax.sharding import PartitionSpec as P


D = 5120
BLOCK = 108


def block_slots(keep_mask, slot_count):
    positions = jnp.arange(keep_mask.shape[0], dtype=jnp.int32)
    ranking = jnp.cumsum(keep_mask) - 1
    slot_ids = jnp.arange(slot_count, dtype=jnp.int32)
    matches = keep_mask[None, :] * (ranking[None, :] == slot_ids[:, None]).astype(jnp.int32)
    block_index = jnp.sum(matches * positions[None, :], axis=1)
    block_live = jnp.sum(matches, axis=1)
    return (block_index, block_live)


def pick_blocks(matrix, block_index, block_live, dim_axis):
    if dim_axis == 1:
        grouped = matrix.reshape(matrix.shape[0], -1, BLOCK)
        picked = jnp.take(grouped, block_index, axis=1) * block_live[None, :, None].astype(
            matrix.dtype
        )
        return picked.reshape(matrix.shape[0], -1)
    grouped = matrix.reshape(-1, BLOCK, matrix.shape[1])
    picked = jnp.take(grouped, block_index, axis=0) * block_live[:, None, None].astype(matrix.dtype)
    return picked.reshape(-1, matrix.shape[1])


def per_device(tokens, w_gate, w_up, w_down, keep_a, keep_b):
    gathered = lax.all_to_all(tokens, "rep", split_axis=1, concat_axis=0, tiled=True)
    part_gate = jnp.dot(gathered, w_gate, preferred_element_type=jnp.float32)
    part_up = jnp.dot(gathered, w_up, preferred_element_type=jnp.float32)
    gate_value, up_value = lax.psum((part_gate, part_up), ("width", "rep"))
    sigmoid_term = jax.nn.sigmoid(gate_value)
    activation = gate_value * sigmoid_term
    slope_term = sigmoid_term * (1.0 + gate_value * (1.0 - sigmoid_term))
    hidden = (activation * up_value).astype(jnp.bfloat16)
    shard_blocks = keep_a.shape[0]
    variant_plans = ((keep_a, 3 * shard_blocks // 4), (keep_b, shard_blocks // 2))
    differences = jnp.stack(
        [
            -jnp.dot(
                hidden * (1 - jnp.repeat(keep_mask, BLOCK)).astype(jnp.bfloat16)[None, :],
                w_down,
                preferred_element_type=jnp.float32,
            )
            for keep_mask, slot_count in variant_plans
        ]
    )
    scale_count = gathered.shape[0] * D
    totals = lax.psum(differences, "hidden")
    squares = jnp.sum(totals * totals, axis=(1, 2))
    losses = lax.psum(squares, ("width", "rep")) / scale_count
    errors = totals.astype(jnp.bfloat16)
    slot_plans = [block_slots(keep_mask, slot_count) for keep_mask, slot_count in variant_plans]
    back_terms = [
        jnp.einsum(
            "td,fd->tf",
            errors[variant],
            pick_blocks(w_down, slot_plans[variant][0], slot_plans[variant][1], 0),
            preferred_element_type=jnp.float32,
        )
        for variant in range(2)
    ]
    back_a, back_b = lax.psum((back_terms[0], back_terms[1]), ("width", "rep"))
    results = []
    for variant, back_total in ((0, back_a), (1, back_b)):
        block_index, block_live = slot_plans[variant]
        keep_mask = variant_plans[variant][0]
        up_slot = pick_blocks(up_value, block_index, block_live, 1)
        slope_slot = pick_blocks(slope_term, block_index, block_live, 1)
        act_slot = pick_blocks(activation, block_index, block_live, 1)
        hidden_slot = pick_blocks(hidden, block_index, block_live, 1)
        delta_gate = (back_total * up_slot * slope_slot).astype(jnp.bfloat16)
        delta_up = (back_total * act_slot).astype(jnp.bfloat16)
        grad_gate = jnp.einsum(
            "td,tf->df", gathered, delta_gate, preferred_element_type=jnp.float32
        )
        grad_up = jnp.einsum("td,tf->df", gathered, delta_up, preferred_element_type=jnp.float32)
        grad_down = jnp.einsum(
            "tf,td->fd", hidden_slot, errors[variant], preferred_element_type=jnp.float32
        )
        results.append(
            (
                grad_gate.astype(jnp.bfloat16),
                grad_up.astype(jnp.bfloat16),
                grad_down.astype(jnp.bfloat16),
            )
        )
    return (
        results[0][0],
        results[0][1],
        results[0][2],
        results[1][0],
        results[1][1],
        results[1][2],
        losses,
    )


MESH = pl.DeviceIdType.MESH
VMEM_LIMIT = 63 << 20


def nt(a, b):
    return lax.dot_general(a, b, (((1,), (1,)), ((), ())), preferred_element_type=jnp.float32)


def nn(a, b):
    return jnp.dot(a, b, preferred_element_type=jnp.float32)


def forward_kernel(
    chunks, block, slots,
    tok_hbm, wg_hbm, wu_hbm, wd_hbm, keep_a_ref, keep_b_ref,
    err_hbm, hid_hbm, act_hbm, fac_hbm, tok_out, sq_ref, plan_ref,
    tok, wgb, wub, wd, part, stage, ring, xs, xr, hid, lhs, zp, zs, zr, errs, mask_ref,
    tok_s, tok_r, w_sem, wd_sem, st_s, ring_r, x_s, x_r, hid_s, hid_r, z_s, z_r, keep_s, err_s,
):
    n = lax.axis_size("hidden")
    z, wide, core = lax.axis_index("hidden"), lax.axis_index("width"), lax.axis_index("rep")
    depth, units = wg_hbm.shape
    half = tok_hbm.shape[0]
    blocks = units // block
    partner, across = {"rep": 1 - core}, {"width": 1 - wide}

    def local(src, dst, sem):
        return pltpu.make_async_copy(src, dst, sem)

    def remote(src, dst, ssem, rsem, peer):
        return pltpu.make_async_remote_copy(
            src, dst, ssem, rsem, device_id=peer, device_id_type=MESH
        )

    def weights(j):
        lanes = pl.ds(pl.multiple_of(j * block, 128), block)
        slot = lax.rem(j, 2)
        return (
            local(wg_hbm.at[:, lanes], wgb.at[slot], w_sem.at[0, slot]),
            local(wu_hbm.at[:, lanes], wub.at[slot], w_sem.at[1, slot]),
        )

    for j in range(2):
        for copy in weights(j):
            copy.start()
    mine = local(
        tok_hbm.at[:, pl.ds(pl.multiple_of(core * depth, 128), depth)], tok.at[0], wd_sem
    )
    mine.start()
    load_down = local(wd_hbm, wd, wd_sem)

    barrier = pltpu.get_barrier_semaphore()
    pl.semaphore_signal(barrier, inc=1, device_id=partner, device_id_type=MESH)
    pl.semaphore_signal(barrier, inc=1, device_id=across, device_id_type=MESH)

    @pl.when(z > 0)
    def _():
        pl.semaphore_signal(barrier, inc=1, device_id={"hidden": z - 1}, device_id_type=MESH)

    @pl.when(z < n - 1)
    def _():
        pl.semaphore_signal(barrier, inc=1, device_id={"hidden": z + 1}, device_id_type=MESH)

    @pl.when((z == 0) | (z == n - 1))
    def _():
        pl.semaphore_wait(barrier, 3)

    @pl.when((z > 0) & (z < n - 1))
    def _():
        pl.semaphore_wait(barrier, 4)

    give = remote(
        tok_hbm.at[:, pl.ds(pl.multiple_of((1 - core) * depth, 128), depth)],
        tok.at[1], tok_s, tok_r, partner,
    )
    give.start()
    sq_ref[...] = jnp.zeros_like(sq_ref)
    shard_blocks = keep_a_ref.shape[0]
    keeps = (keep_a_ref, keep_b_ref)
    unit = lax.broadcasted_iota(jnp.int32, (1, units), 1)
    for k, keep in enumerate(keeps):
        level = jnp.zeros((1, units), jnp.float32)
        before = 1
        for b in range(shard_blocks):
            jump = (keep[b] - before).astype(jnp.float32)
            level = level + jnp.where(unit >= b * BLOCK, jump, 0.0)
            before = keep[b]
        mask_ref[k : k + 1, :] = level
    slot = lax.broadcasted_iota(jnp.int32, (1, 128), 1)
    start, live = jnp.zeros((1, 128), jnp.int32), jnp.zeros((1, 128), jnp.int32)
    base = 0
    for keep, count in zip(keeps, slots):
        seen = base
        for b in range(shard_blocks):
            hit = jnp.where(slot == seen, keep[b], 0)
            live = live + hit
            start = start + hit * (b * BLOCK)
            seen = seen + keep[b]
        base += count
    plan_ref[0:1, :] = start
    plan_ref[1:2, :] = live
    mine.wait()
    give.wait()
    load_down.start()
    keep_tok = local(tok, tok_out, tok_s)
    keep_tok.start()

    def push(j):
        return remote(
            stage.at[lax.rem(j, 2)], ring.at[lax.rem(j, 4)],
            st_s.at[lax.rem(j, 2)], ring_r.at[lax.rem(j, 4)], partner,
        )

    first = chunks[0][1]

    def cross_block(j):
        lanes = pl.ds(pl.multiple_of(j * block, 128), block)
        return remote(
            xs.at[:, pl.ds(0, first), lanes], xr.at[:, pl.ds(0, first), lanes],
            x_s.at[0], x_r.at[0], across,
        )

    def cross(c):
        rows = pl.ds(*chunks[c])
        return remote(xs.at[:, rows, :], xr.at[:, rows, :], x_s.at[c], x_r.at[c], across)

    def take(j):
        lanes = pl.ds(pl.multiple_of(j * block, 128), block)
        slot = lax.rem(j, 4)
        push(j).wait_recv()
        for i in range(2):
            total = part[i, :, lanes] + ring[slot, i]
            part[i, :, lanes] = total
            xs[i, :, lanes] = total.astype(jnp.bfloat16)
        cross_block(j).start()

    def step(j, carry):
        for copy in weights(j):
            copy.wait()
        slot = lax.rem(j, 2)
        lanes = pl.ds(pl.multiple_of(j * block, 128), block)

        @pl.when(j >= 2)
        def _():
            push(j).wait_send()

        stage[slot, 0] = nn(tok[1], wgb[slot])
        stage[slot, 1] = nn(tok[1], wub[slot])
        push(j).start()

        @pl.when(j >= 1)
        def _():
            take(j - 1)

        part[0, :, lanes] = nn(tok[0], wgb[slot])
        part[1, :, lanes] = nn(tok[0], wub[slot])

        @pl.when(j + 2 < blocks)
        def _():
            for copy in weights(j + 2):
                copy.start()

        return carry

    lax.fori_loop(0, blocks, step, 0)
    take(blocks - 1)
    for c in range(1, len(chunks)):
        cross(c).start()
    for j in (blocks - 2, blocks - 1):
        push(j).wait_send()
    load_down.wait()

    def swap_hidden(c):
        rows = pl.ds(*chunks[c])
        return remote(hid.at[0, rows], hid.at[1, rows], hid_s.at[c], hid_r.at[c], partner)

    def keep_out(c):
        rows = pl.ds(*chunks[c])
        return (
            local(part.at[0, rows], act_hbm.at[rows], keep_s.at[0, c]),
            local(part.at[1, rows], fac_hbm.at[rows], keep_s.at[1, c]),
        )

    def activate(c):
        start, count = chunks[c]
        rows = pl.ds(start, count)
        cross(c).wait_recv()

        def lane_block(j, carry):
            lanes = pl.ds(pl.multiple_of(j * block, 128), block)
            gate = part[0, rows, lanes] + xr[0, rows, lanes].astype(jnp.float32)
            up = part[1, rows, lanes] + xr[1, rows, lanes].astype(jnp.float32)
            sigmoid = jax.nn.sigmoid(gate)
            act = gate * sigmoid
            hid[0, rows, lanes] = (act * up).astype(jnp.bfloat16)
            part[0, rows, lanes] = act
            part[1, rows, lanes] = up * (sigmoid * (1.0 + gate * (1.0 - sigmoid)))
            return carry

        lax.fori_loop(0, blocks, lane_block, 0)
        swap_hidden(c).start()
        for copy in keep_out(c):
            copy.start()

    def hid_out(c):
        rows = pl.ds(*chunks[c])
        return local(hid.at[:, rows], hid_hbm.at[:, rows], keep_s.at[2, c])

    def differ(c):
        start, count = chunks[c]
        rows = pl.ds(start, count)
        swap_hidden(c).wait_recv()
        hid_out(c).start()

        def masked(j, carry):
            lanes = pl.ds(pl.multiple_of(j * block, 128), block)
            for side in range(2):
                value = hid[side, rows, lanes]
                for k in range(2):
                    drop = mask_ref[k : k + 1, lanes].astype(jnp.bfloat16)
                    lhs[pl.ds((2 * k + side) * count, count), lanes] = value * drop
            return carry

        lax.fori_loop(0, blocks, masked, 0)

        def columns(j, carry):
            lanes = pl.ds(pl.multiple_of(j * 256, 128), 256)
            zp[pl.ds(4 * start, 4 * count), lanes] = nn(lhs[pl.ds(0, 4 * count), :], wd[:, lanes])
            return carry

        lax.fori_loop(0, depth // 256, columns, 0)

    def z_copy(c, d, q):
        start, count = chunks[c]
        rows = pl.ds(pl.multiple_of(4 * start + q * count, 16), count)
        peer = {"hidden": z + 1 - 2 * d}
        return remote(zs.at[d, rows], zr.at[d, rows], z_s.at[c, d, q], z_r.at[c, d, q], peer)

    def has_up(d):
        return ((d == 0) & (z > 0)) | ((d == 1) & (z < n - 1))

    def has_down(d):
        return ((d == 0) & (z < n - 1)) | ((d == 1) & (z > 0))

    def hop(c, d, q):
        start, count = chunks[c]
        rows = pl.ds(pl.multiple_of(4 * start + q * count, 16), count)

        @pl.when(has_up(d))
        def _():
            z_copy(c, d, q).wait_recv()

        @pl.when(has_up(d) & has_down(d))
        def _():
            total = zp[rows, :] + zr[d, rows, :].astype(jnp.float32)
            zs[d, rows, :] = total.astype(jnp.bfloat16)

        @pl.when(has_down(d) & jnp.logical_not(has_up(d)))
        def _():
            zs[d, rows, :] = zp[rows, :].astype(jnp.bfloat16)

        @pl.when(has_down(d))
        def _():
            z_copy(c, d, q).start()

    def err_out(c, q):
        start, count = chunks[c]
        rows = pl.ds(pl.multiple_of(4 * start + q * count, 16), count)
        return local(errs.at[rows], err_hbm.at[q, pl.ds(start, count)], err_s.at[c, q])

    def finish(c, q):
        start, count = chunks[c]
        rows = pl.ds(pl.multiple_of(4 * start + q * count, 16), count)

        def settle(total):
            errs[rows, :] = total.astype(jnp.bfloat16)
            square = total * total
            folded = square[0:8]
            for i in range(8, count, 8):
                folded = folded + square[i : i + 8]
            narrow = folded[:, 0:128]
            for i in range(128, depth, 128):
                narrow = narrow + folded[:, i : i + 128]
            k = q // 2
            sq_ref[k] = sq_ref[k] + narrow

        @pl.when(z == 0)
        def _():
            settle(zp[rows, :] + zr[1, rows, :].astype(jnp.float32))

        @pl.when(z == n - 1)
        def _():
            settle(zp[rows, :] + zr[0, rows, :].astype(jnp.float32))

        @pl.when((z > 0) & (z < n - 1))
        def _():
            settle(
                zp[rows, :]
                + (zr[0, rows, :].astype(jnp.float32) + zr[1, rows, :].astype(jnp.float32))
            )

        err_out(c, q).start()

    early = (2 * z) // n
    late = 1 - early
    edge = (z == 0) | (z == n - 1)
    last = len(chunks) - 1

    def each(first, end, *actions):
        def piece(q, carry):
            for action, c, args in actions:
                action(c, *args, q)
            return carry

        lax.fori_loop(first, end, piece, 0)

    for c in range(len(chunks)):
        activate(c)
        differ(c)

        @pl.when(edge)
        def _(c=c):
            each(0, 4, (hop, c, (early,)))
            if c > 1:
                each(0, 4, (hop, c - 2, (late,)), (finish, c - 2, ()))

        @pl.when(jnp.logical_not(edge))
        def _(c=c):
            if c > 0:
                each(2, 4, (hop, c - 1, (early,)))
                each(0, 2, (hop, c - 1, (late,)), (finish, c - 1, ()))
            each(0, 2, (hop, c, (early,)))
            if c > 0:
                each(2, 4, (hop, c - 1, (late,)), (finish, c - 1, ()))

    @pl.when(edge)
    def _():
        each(0, 4, (hop, last - 1, (late,)), (finish, last - 1, ()))

    @pl.when(jnp.logical_not(edge))
    def _():
        each(2, 4, (hop, last, (early,)))

    each(0, 4, (hop, last, (late,)), (finish, last, ()))

    keep_tok.wait()
    for c in range(len(chunks)):
        cross(c).wait_send()
        swap_hidden(c).wait_send()
        hid_out(c).wait()
        for copy in keep_out(c):
            copy.wait()

        def drain(q, carry, c=c):
            err_out(c, q).wait()
            for d in range(2):
                @pl.when(has_down(d))
                def _():
                    z_copy(c, d, q).wait_send()
            return carry

        lax.fori_loop(0, 4, drain, 0)


def forward_call(slots, tokens, w_gate, w_up, w_down, keep_a, keep_b):
    half, (depth, units) = tokens.shape[0], w_gate.shape
    block = 384 if units % 384 == 0 else 128
    counts = [half * part // 16 for part in (4, 3, 3, 2, 2, 2)]
    chunks = tuple((sum(counts[:i]), count) for i, count in enumerate(counts))
    parts = len(chunks)
    bf, f32 = jnp.bfloat16, jnp.float32
    anywhere = pl.BlockSpec(memory_space=pl.ANY)
    vmem = pl.BlockSpec(memory_space=pltpu.VMEM)
    smem = pl.BlockSpec(memory_space=pltpu.SMEM)
    dma = pltpu.SemaphoreType.DMA
    return pl.pallas_call(
        functools.partial(forward_kernel, chunks, block, slots),
        out_shape=(
            jax.ShapeDtypeStruct((4, half, depth), bf),
            jax.ShapeDtypeStruct((2, half, units), bf),
            jax.ShapeDtypeStruct((half, units), f32),
            jax.ShapeDtypeStruct((half, units), f32),
            jax.ShapeDtypeStruct((2, half, depth), bf),
            jax.ShapeDtypeStruct((2, 8, 128), f32),
            jax.ShapeDtypeStruct((2, 128), jnp.int32),
        ),
        in_specs=[anywhere] * 4 + [smem] * 2,
        out_specs=(anywhere,) * 5 + (vmem,) * 2,
        scratch_shapes=[
            pltpu.VMEM((2, half, depth), bf),
            pltpu.VMEM((2, depth, block), bf),
            pltpu.VMEM((2, depth, block), bf),
            pltpu.VMEM((units, depth), bf),
            pltpu.VMEM((2, half, units), f32),
            pltpu.VMEM((2, 2, half, block), f32),
            pltpu.VMEM((4, 2, half, block), f32),
            pltpu.VMEM((2, half, units), bf),
            pltpu.VMEM((2, half, units), bf),
            pltpu.VMEM((2, half, units), bf),
            pltpu.VMEM((4 * max(counts), units), bf),
            pltpu.VMEM((4 * half, depth), f32),
            pltpu.VMEM((2, 4 * half, depth), bf),
            pltpu.VMEM((2, 4 * half, depth), bf),
            pltpu.VMEM((4 * half, depth), bf),
            pltpu.VMEM((2, units), f32),
            dma, dma, dma((2, 2)), dma, dma((2,)), dma((4,)),
            dma((parts,)), dma((parts,)), dma((parts,)), dma((parts,)),
            dma((parts, 2, 4)), dma((parts, 2, 4)), dma((3, parts)), dma((parts, 4)),
        ],
        compiler_params=pltpu.CompilerParams(
            collective_id=0, has_side_effects=True, vmem_limit_bytes=VMEM_LIMIT
        ),
    )(tokens, w_gate, w_up, w_down, keep_a, keep_b)


def backward_kernel(
    slots,
    plan_ref, err_hbm, wd_hbm, act_hbm, fac_hbm, hid_hbm, sq_ref,
    dga_hbm, dua_hbm, ha_hbm, dgb_hbm, dub_hbm, hb_hbm, loss_ref,
    wd, err, bt, give, got, own, xs, xr, nat, act_t, fac_t, hidb, outs, hout,
    sq_core, sq_chip, sq_all,
    in_s, give_s, give_r, x_s, x_r, own_s, far_s, far_r, h_s, l_s, l_r, z_s, z_r,
):
    n = lax.axis_size("hidden")
    z, wide, core = lax.axis_index("hidden"), lax.axis_index("width"), lax.axis_index("rep")
    units, depth = wd_hbm.shape
    half = act_hbm.shape[0]
    pairs = half // 128
    slots_a, slots_b = slots
    rows_a, rows = slots_a * BLOCK, (slots_a + slots_b) * BLOCK
    partner, across = {"rep": 1 - core}, {"width": 1 - wide}

    def local(src, dst, sem):
        return pltpu.make_async_copy(src, dst, sem)

    def remote(src, dst, ssem, rsem, peer):
        return pltpu.make_async_remote_copy(
            src, dst, ssem, rsem, device_id=peer, device_id_type=MESH
        )

    load_err = local(err_hbm, err, in_s.at[0])
    load_act = local(act_hbm, nat, in_s.at[1])
    load_hid = local(hid_hbm.at[0], hidb, in_s.at[2])
    tile = units // 3

    def load_down(i):
        at = pl.ds(pl.multiple_of(i * tile, 128), tile)
        return local(wd_hbm.at[at], wd.at[at], in_s.at[3 + i])

    load_err.start()
    for i in range(3):
        load_down(i).start()

    barrier = pltpu.get_barrier_semaphore()
    pl.semaphore_signal(barrier, inc=1, device_id=partner, device_id_type=MESH)
    pl.semaphore_signal(barrier, inc=1, device_id=across, device_id_type=MESH)
    for k in range(1, n):
        peer = {"hidden": lax.rem(z + k, n)}
        pl.semaphore_signal(barrier, inc=1, device_id=peer, device_id_type=MESH)
    pl.semaphore_wait(barrier, n + 1)
    loss_core = remote(sq_ref, sq_core, l_s.at[0], l_r.at[0], partner)
    loss_chip = remote(loss_ref, sq_chip, l_s.at[1], l_r.at[1], across)
    loss_core.start()

    def fill(side, p):
        lanes = pl.ds(p * 128, 128)
        rhs = jnp.concatenate([err[side, lanes, :], err[2 + side, lanes, :]], axis=0)

        def piece(i, carry):
            if side == 1 and p == 0:
                load_down(i).wait()
            at = pl.ds(pl.multiple_of(i * tile, 128), tile)
            back = nt(wd[at, :], rhs)
            bt[0, at, :] = back[:, 0:128]
            bt[1, at, :] = back[:, 128:256]
            return carry

        lax.fori_loop(0, 3, piece, 0)

    def per_slot(first, count, action):
        def two(i, carry):
            for k in range(2):
                s = first + 2 * i + k
                base = pl.multiple_of((first + 2 * i) * BLOCK, 8) + k * BLOCK
                action(s, pl.ds(plan_ref[0, s], BLOCK), pl.ds(base, BLOCK))
            return carry

        lax.fori_loop(0, count // 2, two, 0)

    counts = ((0, slots_a), (slots_a, slots_b))
    spans = (pl.ds(0, rows_a), pl.ds(rows_a, rows - rows_a))

    def pick(target, v):
        def take(s, source, place):
            target[place, :] = bt[v, source, :]

        per_slot(*counts[v], take)

    strip = BLOCK * 4

    def strips(v, action):
        base = (0, rows_a)[v]

        def step(i, carry):
            action(pl.ds(pl.multiple_of(base + i * strip, 16), strip))
            return carry

        lax.fori_loop(0, (rows_a, rows - rows_a)[v] // strip, step, 0)

    def push(p, v):
        return remote(
            give.at[p, spans[v]], got.at[p, spans[v]], give_s.at[p, v], give_r.at[p, v], partner
        )

    def cross(p, v):
        return remote(xs.at[p, spans[v]], xr.at[p, spans[v]], x_s.at[p, v], x_r.at[p, v], across)

    load_err.wait()
    for p in range(pairs):
        fill(1, p)
        for v in range(2):
            pick(give.at[p], v)
            push(p, v).start()
        if p == 0:
            load_act.start()
            load_hid.start()
            loss_core.wait()
            loss_ref[...] = sq_ref[...] + sq_core[...]
            loss_chip.start()
        fill(0, p)
        for v in range(2):
            pick(own.at[p], v)
            push(p, v).wait_recv()

            def join(at, p=p):
                total = own[p, at, :] + got[p, at, :]
                own[p, at, :] = total
                xs[p, at, :] = total.astype(jnp.bfloat16)

            strips(v, join)
            cross(p, v).start()

    def flip(source, target, count):
        def step(j, carry):
            lanes = pl.ds(pl.multiple_of(j * 128, 128), 128)
            value = source(lanes).astype(jnp.float32).T.astype(target.dtype)
            if len(target.shape) == 2:
                target[lanes, :] = value
            else:
                for i in range(target.shape[0]):
                    target[i, lanes, :] = value[:, i * 128 : (i + 1) * 128]
            return carry

        lax.fori_loop(0, count // 128, step, 0)

    load_act.wait()
    flip(lambda lanes: nat[:, lanes], act_t, units)
    load_fac = local(fac_hbm, nat, in_s.at[1])
    load_fac.start()
    load_fac.wait()
    flip(lambda lanes: nat[:, lanes], fac_t, units)

    loss_chip.wait()
    sq_all[z] = loss_ref[...] + sq_chip[...]

    def share(k):
        return remote(
            sq_all.at[z], sq_all.at[z], z_s.at[k], z_r.at[z],
            {"hidden": lax.rem(z + k, n)},
        )

    for k in range(1, n):
        share(k).start()

    for p in range(pairs):
        for v in range(2):
            push(p, v).wait_send()

    def keep(s, value):
        return jnp.where(plan_ref[1, s] > 0, value, jnp.zeros_like(value))

    def hid_out(side, p):
        lanes = pl.ds(side * half + p * 128, 128)
        return (
            local(hout.at[side, p, pl.ds(0, rows_a)], ha_hbm.at[:, lanes], h_s.at[0, side, p]),
            local(
                hout.at[side, p, pl.ds(rows_a, rows - rows_a)], hb_hbm.at[:, lanes],
                h_s.at[1, side, p],
            ),
        )

    for side in range(2):
        if side == 0:
            load_hid.wait()
        else:
            next_hid = local(hid_hbm.at[1], hidb, in_s.at[2])
            next_hid.start()
            next_hid.wait()
        flip(lambda lanes: hidb[:, lanes], bt, units)
        for p in range(pairs):
            def copy_rows(s, source, place, p=p):
                give[p, place, :] = keep(s, bt[p, source, :])

            per_slot(0, slots_a + slots_b, copy_rows)

            def narrow(at, p=p, side=side):
                hout[side, p, at, :] = give[p, at, :].astype(jnp.bfloat16)

            for v in range(2):
                strips(v, narrow)
            for copy in hid_out(side, p):
                copy.start()

    def delta_out(p, kind, v):
        near = pl.ds(p * 128, 128)
        far = pl.ds(half + p * 128, 128)
        source = outs.at[p, kind, spans[v]]
        target = ((dga_hbm, dgb_hbm), (dua_hbm, dub_hbm))[kind][v]
        return (
            remote(
                source, target.at[:, far], far_s.at[p, kind, v], far_r.at[p, kind, v], partner
            ),
            local(source, target.at[:, near], own_s.at[p, kind, v]),
        )

    for p in range(pairs):
        for v in range(2):
            cross(p, v).wait_recv()

            def combine(at, p=p):
                own[p, at, :] = own[p, at, :] + xr[p, at, :].astype(jnp.float32)

            strips(v, combine)

            def scale(s, source, place, p=p):
                total = keep(s, own[p, place, :])
                got[0, place, :] = total * fac_t[p, source, :]
                got[1, place, :] = total * act_t[p, source, :]

            per_slot(*counts[v], scale)
            for kind in range(2):
                def narrow(at, p=p, kind=kind):
                    outs[p, kind, at, :] = got[kind, at, :].astype(jnp.bfloat16)

                strips(v, narrow)
                for copy in delta_out(p, kind, v):
                    copy.start()

    total = None
    for i in range(n):
        @pl.when(z != i)
        def _(i=i):
            remote(
                sq_all.at[i], sq_all.at[i], z_s.at[0], z_r.at[i], partner
            ).wait_recv()

    for i in range(n):
        total = sq_all[i] if total is None else total + sq_all[i]
    loss_ref[...] = total

    for k in range(1, n):
        share(k).wait_send()
    for p in range(pairs):
        for v in range(2):
            cross(p, v).wait_send()
            for kind in range(2):
                for copy in delta_out(p, kind, v):
                    copy.wait()
        for side in range(2):
            for copy in hid_out(side, p):
                copy.wait()


def backward_call(plan, slots, err, w_down, act, fac, hid, squares):
    (half, units), depth = act.shape, w_down.shape[1]
    rows_a, rows_b = slots[0] * BLOCK, slots[1] * BLOCK
    rows, pairs, n = rows_a + rows_b, half // 128, lax.axis_size("hidden")
    bf, f32 = jnp.bfloat16, jnp.float32
    anywhere = pl.BlockSpec(memory_space=pl.ANY)
    vmem = pl.BlockSpec(memory_space=pltpu.VMEM)
    smem = pl.BlockSpec(memory_space=pltpu.SMEM)
    dma = pltpu.SemaphoreType.DMA
    shape = jax.ShapeDtypeStruct
    return pl.pallas_call(
        functools.partial(backward_kernel, slots),
        out_shape=(
            (shape((rows_a, 2 * half), bf),) * 3
            + (shape((rows_b, 2 * half), bf),) * 3
            + (shape((2, 8, 128), f32),)
        ),
        in_specs=[smem] + [anywhere] * 5 + [vmem],
        out_specs=(anywhere,) * 6 + (vmem,),
        scratch_shapes=[
            pltpu.VMEM((units, depth), bf),
            pltpu.VMEM((4, half, depth), bf),
            pltpu.VMEM((2, units, 128), f32),
            pltpu.VMEM((pairs, rows, 128), f32),
            pltpu.VMEM((pairs, rows, 128), f32),
            pltpu.VMEM((pairs, rows, 128), f32),
            pltpu.VMEM((pairs, rows, 128), bf),
            pltpu.VMEM((pairs, rows, 128), bf),
            pltpu.VMEM((half, units), f32),
            pltpu.VMEM((pairs, units, 128), f32),
            pltpu.VMEM((pairs, units, 128), f32),
            pltpu.VMEM((half, units), bf),
            pltpu.VMEM((pairs, 2, rows, 128), bf),
            pltpu.VMEM((2, pairs, rows, 128), bf),
            pltpu.VMEM((2, 8, 128), f32),
            pltpu.VMEM((2, 8, 128), f32),
            pltpu.VMEM((n, 2, 8, 128), f32),
            dma((6,)), dma((pairs, 2)), dma((pairs, 2)), dma((pairs, 2)), dma((pairs, 2)),
            dma((pairs, 2, 2)), dma((pairs, 2, 2)), dma((pairs, 2, 2)), dma((2, 2, pairs)),
            dma((2,)), dma((2,)), dma((n,)), dma((n,)),
        ],
        compiler_params=pltpu.CompilerParams(
            collective_id=1, has_side_effects=True, vmem_limit_bytes=VMEM_LIMIT
        ),
    )(plan, err, w_down, act, fac, hid, squares)


def gradient_kernel(
    scale,
    dga, dua, ha, dgb, dub, hb, tok, err, sums_ref,
    gga, gua, gda, ggb, gub, gdb, loss_ref,
    left_a, left_b, right, buffer, in_s, out_s,
):
    pieces = 2
    phases = (
        (dga, left_a.at[0], 0, gga), (dua, left_a.at[1], 0, gua), (ha, left_a.at[2], 1, gda),
        (dgb, left_b.at[0], 0, ggb), (dub, left_b.at[1], 0, gub), (hb, left_b.at[2], 2, gdb),
    )
    sources = [(tok, right.at[0])] + [phase[:2] for phase in phases]
    sources.insert(3, (err.at[0], right.at[1]))
    sources.append((err.at[1], right.at[2]))
    loads = [
        pltpu.make_async_copy(src, dst, in_s.at[i]) for i, (src, dst) in enumerate(sources)
    ]
    for load in loads:
        load.start()
    needs = ((0, 1), (2,), (3, 4), (5,), (6,), (7, 8))

    for k in range(2):
        loss_ref[k] = jnp.sum(sums_ref[k]) * scale
    pending = []
    for (_, left, side, out), which in zip(phases, needs):
        for i in which:
            loads[i].wait()
        rows = left.shape[0] // pieces
        for i in range(pieces):
            slot = len(pending) % 2
            if len(pending) > 1:
                pending[-2].wait()
            at = pl.ds(i * rows, rows)
            buffer[slot, pl.ds(0, rows), :] = nn(left[at, :], right[side]).astype(jnp.bfloat16)
            copy = pltpu.make_async_copy(
                buffer.at[slot, pl.ds(0, rows)], out.at[at], out_s.at[slot]
            )
            copy.start()
            pending.append(copy)
    for copy in pending[-2:]:
        copy.wait()


def gradient_call(scale, dga, dua, ha, dgb, dub, hb, tok, err, sums):
    tokens, depth = tok.shape
    rows_a, rows_b = dga.shape[0], dgb.shape[0]
    bf = jnp.bfloat16
    anywhere = pl.BlockSpec(memory_space=pl.ANY)
    dma = pltpu.SemaphoreType.DMA
    flops = 6 * depth * tokens * (rows_a + rows_b)
    gga, gua, gda, ggb, gub, gdb, losses = pl.pallas_call(
        functools.partial(gradient_kernel, scale),
        out_shape=tuple(
            jax.ShapeDtypeStruct((rows, depth), bf) for rows in (rows_a,) * 3 + (rows_b,) * 3
        ) + (jax.ShapeDtypeStruct((2,), jnp.float32),),
        in_specs=[anywhere] * 8 + [pl.BlockSpec(memory_space=pltpu.VMEM)],
        out_specs=(anywhere,) * 6 + (pl.BlockSpec(memory_space=pltpu.SMEM),),
        scratch_shapes=[
            pltpu.VMEM((3, rows_a, tokens), bf),
            pltpu.VMEM((3, rows_b, tokens), bf),
            pltpu.VMEM((3, tokens, depth), bf),
            pltpu.VMEM((2, rows_a // 2, depth), bf),
            dma((9,)), dma((2,)),
        ],
        compiler_params=pltpu.CompilerParams(vmem_limit_bytes=VMEM_LIMIT),
        cost_estimate=pl.CostEstimate(
            flops=flops, bytes_accessed=4 * depth * (rows_a + rows_b) * 2, transcendentals=0
        ),
    )(dga, dua, ha, dgb, dub, hb, tok, err, sums)
    return gga.T, gua.T, gda, ggb.T, gub.T, gdb, losses


def per_device_fast(tokens, w_gate, w_up, w_down, keep_a, keep_b):
    shard_blocks = keep_a.shape[0]
    slots = (3 * shard_blocks // 4, shard_blocks // 2)
    err, hid, act, fac, tok, squares, plan = forward_call(
        slots, tokens, w_gate, w_up, w_down, keep_a, keep_b
    )
    *deltas, sums = backward_call(plan, slots, err, w_down, act, fac, hid, squares)
    token_count = 2 * tokens.shape[0]
    scale = 1.0 / (lax.axis_size("hidden") * token_count * D)
    return gradient_call(
        scale, *deltas, tok.reshape(token_count, -1), err.reshape(2, token_count, -1), sums
    )


def solution(mesh):
    in_specs = (
        P(("groups", "rep"), "width"),
        P(("width", "rep"), "hidden"),
        P(("width", "rep"), "hidden"),
        P("hidden", ("width", "rep")),
        P("hidden"),
        P("hidden"),
    )
    out_specs = (
        P(("width", "rep"), ("groups", "hidden")),
        P(("width", "rep"), ("groups", "hidden")),
        P(("groups", "hidden"), ("width", "rep")),
        P(("width", "rep"), ("groups", "hidden")),
        P(("width", "rep"), ("groups", "hidden")),
        P(("groups", "hidden"), ("width", "rep")),
        P("groups"),
    )
    sizes = mesh.shape
    body = per_device
    if sizes["width"] == 2 and sizes["rep"] == 2 and 2 <= sizes["hidden"] <= 4:
        body = per_device_fast
    return jax.shard_map(
        body, mesh=mesh, in_specs=in_specs, out_specs=out_specs, check_vma=False
    )
```

```python
import functools

import jax
import jax.numpy as jnp
from jax import lax
from jax.experimental import pallas as pl
from jax.experimental.pallas import tpu as pltpu
from jax.sharding import PartitionSpec as P


D = 5120
BLOCK = 108


def block_slots(keep_mask, slot_count):
    positions = jnp.arange(keep_mask.shape[0], dtype=jnp.int32)
    ranking = jnp.cumsum(keep_mask) - 1
    slot_ids = jnp.arange(slot_count, dtype=jnp.int32)
    matches = keep_mask[None, :] * (ranking[None, :] == slot_ids[:, None]).astype(jnp.int32)
    block_index = jnp.sum(matches * positions[None, :], axis=1)
    block_live = jnp.sum(matches, axis=1)
    return (block_index, block_live)


def pick_blocks(matrix, block_index, block_live, dim_axis):
    if dim_axis == 1:
        grouped = matrix.reshape(matrix.shape[0], -1, BLOCK)
        picked = jnp.take(grouped, block_index, axis=1) * block_live[None, :, None].astype(
            matrix.dtype
        )
        return picked.reshape(matrix.shape[0], -1)
    grouped = matrix.reshape(-1, BLOCK, matrix.shape[1])
    picked = jnp.take(grouped, block_index, axis=0) * block_live[:, None, None].astype(matrix.dtype)
    return picked.reshape(-1, matrix.shape[1])


def per_device(tokens, w_gate, w_up, w_down, keep_a, keep_b):
    gathered = lax.all_to_all(tokens, "rep", split_axis=1, concat_axis=0, tiled=True)
    part_gate = jnp.dot(gathered, w_gate, preferred_element_type=jnp.float32)
    part_up = jnp.dot(gathered, w_up, preferred_element_type=jnp.float32)
    gate_value, up_value = lax.psum((part_gate, part_up), ("width", "rep"))
    sigmoid_term = jax.nn.sigmoid(gate_value)
    activation = gate_value * sigmoid_term
    slope_term = sigmoid_term * (1.0 + gate_value * (1.0 - sigmoid_term))
    hidden = (activation * up_value).astype(jnp.bfloat16)
    shard_blocks = keep_a.shape[0]
    variant_plans = ((keep_a, 3 * shard_blocks // 4), (keep_b, shard_blocks // 2))
    differences = jnp.stack(
        [
            -jnp.dot(
                hidden * (1 - jnp.repeat(keep_mask, BLOCK)).astype(jnp.bfloat16)[None, :],
                w_down,
                preferred_element_type=jnp.float32,
            )
            for keep_mask, slot_count in variant_plans
        ]
    )
    scale_count = gathered.shape[0] * D
    totals = lax.psum(differences, "hidden")
    squares = jnp.sum(totals * totals, axis=(1, 2))
    losses = lax.psum(squares, ("width", "rep")) / scale_count
    errors = totals.astype(jnp.bfloat16)
    slot_plans = [block_slots(keep_mask, slot_count) for keep_mask, slot_count in variant_plans]
    back_terms = [
        jnp.einsum(
            "td,fd->tf",
            errors[variant],
            pick_blocks(w_down, slot_plans[variant][0], slot_plans[variant][1], 0),
            preferred_element_type=jnp.float32,
        )
        for variant in range(2)
    ]
    back_a, back_b = lax.psum((back_terms[0], back_terms[1]), ("width", "rep"))
    results = []
    for variant, back_total in ((0, back_a), (1, back_b)):
        block_index, block_live = slot_plans[variant]
        keep_mask = variant_plans[variant][0]
        up_slot = pick_blocks(up_value, block_index, block_live, 1)
        slope_slot = pick_blocks(slope_term, block_index, block_live, 1)
        act_slot = pick_blocks(activation, block_index, block_live, 1)
        hidden_slot = pick_blocks(hidden, block_index, block_live, 1)
        delta_gate = (back_total * up_slot * slope_slot).astype(jnp.bfloat16)
        delta_up = (back_total * act_slot).astype(jnp.bfloat16)
        grad_gate = jnp.einsum(
            "td,tf->df", gathered, delta_gate, preferred_element_type=jnp.float32
        )
        grad_up = jnp.einsum("td,tf->df", gathered, delta_up, preferred_element_type=jnp.float32)
        grad_down = jnp.einsum(
            "tf,td->fd", hidden_slot, errors[variant], preferred_element_type=jnp.float32
        )
        results.append(
            (
                grad_gate.astype(jnp.bfloat16),
                grad_up.astype(jnp.bfloat16),
                grad_down.astype(jnp.bfloat16),
            )
        )
    return (
        results[0][0],
        results[0][1],
        results[0][2],
        results[1][0],
        results[1][1],
        results[1][2],
        losses,
    )


MESH = pl.DeviceIdType.MESH
VMEM_LIMIT = 63 << 20


def nt(a, b):
    return lax.dot_general(a, b, (((1,), (1,)), ((), ())), preferred_element_type=jnp.float32)


def nn(a, b):
    return jnp.dot(a, b, preferred_element_type=jnp.float32)


def forward_kernel(
    chunks, block, slots,
    tok_hbm, wg_hbm, wu_hbm, wd_hbm, keep_a_ref, keep_b_ref,
    err_hbm, hid_hbm, act_hbm, fac_hbm, tok_out, sq_ref, plan_ref,
    tok, wgb, wub, wd, part, stage, ring, xs, xr, hid, lhs, zp, zs, zr, errs, mask_ref,
    tok_s, tok_r, w_sem, wd_sem, st_s, ring_r, x_s, x_r, hid_s, hid_r, z_s, z_r, keep_s, err_s,
):
    n = lax.axis_size("hidden")
    z, wide, core = lax.axis_index("hidden"), lax.axis_index("width"), lax.axis_index("rep")
    depth, units = wg_hbm.shape
    half = tok_hbm.shape[0]
    blocks = units // block
    partner, across = {"rep": 1 - core}, {"width": 1 - wide}

    def local(src, dst, sem):
        return pltpu.make_async_copy(src, dst, sem)

    def remote(src, dst, ssem, rsem, peer):
        return pltpu.make_async_remote_copy(
            src, dst, ssem, rsem, device_id=peer, device_id_type=MESH
        )

    def weights(j):
        lanes = pl.ds(pl.multiple_of(j * block, 128), block)
        slot = lax.rem(j, 2)
        return (
            local(wg_hbm.at[:, lanes], wgb.at[slot], w_sem.at[0, slot]),
            local(wu_hbm.at[:, lanes], wub.at[slot], w_sem.at[1, slot]),
        )

    for j in range(2):
        for copy in weights(j):
            copy.start()
    mine = local(
        tok_hbm.at[:, pl.ds(pl.multiple_of(core * depth, 128), depth)], tok.at[0], wd_sem
    )
    mine.start()
    load_down = local(wd_hbm, wd, wd_sem)

    barrier = pltpu.get_barrier_semaphore()
    pl.semaphore_signal(barrier, inc=1, device_id=partner, device_id_type=MESH)
    pl.semaphore_signal(barrier, inc=1, device_id=across, device_id_type=MESH)

    @pl.when(z > 0)
    def _():
        pl.semaphore_signal(barrier, inc=1, device_id={"hidden": z - 1}, device_id_type=MESH)

    @pl.when(z < n - 1)
    def _():
        pl.semaphore_signal(barrier, inc=1, device_id={"hidden": z + 1}, device_id_type=MESH)

    @pl.when((z == 0) | (z == n - 1))
    def _():
        pl.semaphore_wait(barrier, 3)

    @pl.when((z > 0) & (z < n - 1))
    def _():
        pl.semaphore_wait(barrier, 4)

    give = remote(
        tok_hbm.at[:, pl.ds(pl.multiple_of((1 - core) * depth, 128), depth)],
        tok.at[1], tok_s, tok_r, partner,
    )
    give.start()
    sq_ref[...] = jnp.zeros_like(sq_ref)
    mine.wait()
    give.wait()
    load_down.start()
    keep_tok = local(tok, tok_out, tok_s)
    keep_tok.start()

    def push(j):
        return remote(
            stage.at[lax.rem(j, 2)], ring.at[lax.rem(j, 4)],
            st_s.at[lax.rem(j, 2)], ring_r.at[lax.rem(j, 4)], partner,
        )

    first = chunks[0][1]

    def cross_block(j):
        lanes = pl.ds(pl.multiple_of(j * block, 128), block)
        return remote(
            xs.at[:, pl.ds(0, first), lanes], xr.at[:, pl.ds(0, first), lanes],
            x_s.at[0], x_r.at[0], across,
        )

    def cross(c):
        rows = pl.ds(*chunks[c])
        return remote(xs.at[:, rows, :], xr.at[:, rows, :], x_s.at[c], x_r.at[c], across)

    def take(j):
        lanes = pl.ds(pl.multiple_of(j * block, 128), block)
        slot = lax.rem(j, 4)
        push(j).wait_recv()
        for i in range(2):
            total = part[i, :, lanes] + ring[slot, i]
            part[i, :, lanes] = total
            xs[i, :, lanes] = total.astype(jnp.bfloat16)
        cross_block(j).start()

    def step(j, carry):
        for copy in weights(j):
            copy.wait()
        slot = lax.rem(j, 2)
        lanes = pl.ds(pl.multiple_of(j * block, 128), block)

        @pl.when(j >= 2)
        def _():
            push(j).wait_send()

        stage[slot, 0] = nn(tok[1], wgb[slot])
        stage[slot, 1] = nn(tok[1], wub[slot])
        push(j).start()

        @pl.when(j >= 1)
        def _():
            take(j - 1)

        part[0, :, lanes] = nn(tok[0], wgb[slot])
        part[1, :, lanes] = nn(tok[0], wub[slot])

        @pl.when(j + 2 < blocks)
        def _():
            for copy in weights(j + 2):
                copy.start()

        return carry

    lax.fori_loop(0, blocks, step, 0)
    take(blocks - 1)
    for c in range(1, len(chunks)):
        cross(c).start()
    for j in (blocks - 2, blocks - 1):
        push(j).wait_send()
    load_down.wait()
    shard_blocks = keep_a_ref.shape[0]
    keeps = (keep_a_ref, keep_b_ref)
    unit = lax.broadcasted_iota(jnp.int32, (1, units), 1)
    for k, keep in enumerate(keeps):
        level = jnp.zeros((1, units), jnp.float32)
        before = 1
        for b in range(shard_blocks):
            jump = (keep[b] - before).astype(jnp.float32)
            level = level + jnp.where(unit >= b * BLOCK, jump, 0.0)
            before = keep[b]
        mask_ref[k : k + 1, :] = level
    slot = lax.broadcasted_iota(jnp.int32, (1, 128), 1)
    start, live = jnp.zeros((1, 128), jnp.int32), jnp.zeros((1, 128), jnp.int32)
    base = 0
    for keep, count in zip(keeps, slots):
        seen = base
        for b in range(shard_blocks):
            hit = jnp.where(slot == seen, keep[b], 0)
            live = live + hit
            start = start + hit * (b * BLOCK)
            seen = seen + keep[b]
        base += count
    plan_ref[0:1, :] = start
    plan_ref[1:2, :] = live

    def swap_hidden(c):
        rows = pl.ds(*chunks[c])
        return remote(hid.at[0, rows], hid.at[1, rows], hid_s.at[c], hid_r.at[c], partner)

    def keep_out(c):
        rows = pl.ds(*chunks[c])
        return (
            local(part.at[0, rows], act_hbm.at[rows], keep_s.at[0, c]),
            local(part.at[1, rows], fac_hbm.at[rows], keep_s.at[1, c]),
        )

    def activate(c):
        start, count = chunks[c]
        rows = pl.ds(start, count)
        cross(c).wait_recv()

        def lane_block(j, carry):
            lanes = pl.ds(pl.multiple_of(j * block, 128), block)
            gate = part[0, rows, lanes] + xr[0, rows, lanes].astype(jnp.float32)
            up = part[1, rows, lanes] + xr[1, rows, lanes].astype(jnp.float32)
            sigmoid = jax.nn.sigmoid(gate)
            act = gate * sigmoid
            hid[0, rows, lanes] = (act * up).astype(jnp.bfloat16)
            part[0, rows, lanes] = act
            part[1, rows, lanes] = up * (sigmoid * (1.0 + gate * (1.0 - sigmoid)))
            return carry

        lax.fori_loop(0, blocks, lane_block, 0)
        swap_hidden(c).start()
        for copy in keep_out(c):
            copy.start()

    def hid_out(c):
        rows = pl.ds(*chunks[c])
        return local(hid.at[:, rows], hid_hbm.at[:, rows], keep_s.at[2, c])

    def differ(c):
        start, count = chunks[c]
        rows = pl.ds(start, count)
        swap_hidden(c).wait_recv()
        hid_out(c).start()

        def masked(j, carry):
            lanes = pl.ds(pl.multiple_of(j * block, 128), block)
            for side in range(2):
                value = hid[side, rows, lanes]
                for k in range(2):
                    drop = mask_ref[k : k + 1, lanes].astype(jnp.bfloat16)
                    lhs[pl.ds((2 * k + side) * count, count), lanes] = value * drop
            return carry

        lax.fori_loop(0, blocks, masked, 0)

        def columns(j, carry):
            lanes = pl.ds(pl.multiple_of(j * 256, 128), 256)
            zp[pl.ds(4 * start, 4 * count), lanes] = nn(lhs[pl.ds(0, 4 * count), :], wd[:, lanes])
            return carry

        lax.fori_loop(0, depth // 256, columns, 0)

    def z_copy(c, d, q):
        start, count = chunks[c]
        rows = pl.ds(pl.multiple_of(4 * start + q * count, 16), count)
        peer = {"hidden": z + 1 - 2 * d}
        return remote(zs.at[d, rows], zr.at[d, rows], z_s.at[c, d, q], z_r.at[c, d, q], peer)

    def has_up(d):
        return ((d == 0) & (z > 0)) | ((d == 1) & (z < n - 1))

    def has_down(d):
        return ((d == 0) & (z < n - 1)) | ((d == 1) & (z > 0))

    def hop(c, d, q):
        start, count = chunks[c]
        rows = pl.ds(pl.multiple_of(4 * start + q * count, 16), count)

        @pl.when(has_up(d))
        def _():
            z_copy(c, d, q).wait_recv()

        @pl.when(has_up(d) & has_down(d))
        def _():
            total = zp[rows, :] + zr[d, rows, :].astype(jnp.float32)
            zs[d, rows, :] = total.astype(jnp.bfloat16)

        @pl.when(has_down(d) & jnp.logical_not(has_up(d)))
        def _():
            zs[d, rows, :] = zp[rows, :].astype(jnp.bfloat16)

        @pl.when(has_down(d))
        def _():
            z_copy(c, d, q).start()

    def err_out(c, q):
        start, count = chunks[c]
        rows = pl.ds(pl.multiple_of(4 * start + q * count, 16), count)
        return local(errs.at[rows], err_hbm.at[q, pl.ds(start, count)], err_s.at[c, q])

    def finish(c, q):
        start, count = chunks[c]
        rows = pl.ds(pl.multiple_of(4 * start + q * count, 16), count)

        def settle(total):
            errs[rows, :] = total.astype(jnp.bfloat16)
            square = total * total
            folded = square[0:8]
            for i in range(8, count, 8):
                folded = folded + square[i : i + 8]
            narrow = folded[:, 0:128]
            for i in range(128, depth, 128):
                narrow = narrow + folded[:, i : i + 128]
            k = q // 2
            sq_ref[k] = sq_ref[k] + narrow

        @pl.when(z == 0)
        def _():
            settle(zp[rows, :] + zr[1, rows, :].astype(jnp.float32))

        @pl.when(z == n - 1)
        def _():
            settle(zp[rows, :] + zr[0, rows, :].astype(jnp.float32))

        @pl.when((z > 0) & (z < n - 1))
        def _():
            settle(
                zp[rows, :]
                + (zr[0, rows, :].astype(jnp.float32) + zr[1, rows, :].astype(jnp.float32))
            )

        err_out(c, q).start()

    early = (2 * z) // n
    late = 1 - early
    edge = (z == 0) | (z == n - 1)
    last = len(chunks) - 1

    def each(first, end, *actions):
        def piece(q, carry):
            for action, c, args in actions:
                action(c, *args, q)
            return carry

        lax.fori_loop(first, end, piece, 0)

    for c in range(len(chunks)):
        activate(c)
        differ(c)

        @pl.when(edge)
        def _(c=c):
            each(0, 4, (hop, c, (early,)))
            if c > 2:
                each(0, 4, (hop, c - 3, (late,)), (finish, c - 3, ()))

        @pl.when(jnp.logical_not(edge))
        def _(c=c):
            if c > 0:
                each(2, 4, (hop, c - 1, (early,)))
                each(0, 2, (hop, c - 1, (late,)), (finish, c - 1, ()))
            each(0, 2, (hop, c, (early,)))
            if c > 0:
                each(2, 4, (hop, c - 1, (late,)), (finish, c - 1, ()))

    @pl.when(edge)
    def _():
        each(0, 4, (hop, last - 2, (late,)), (finish, last - 2, ()))
        each(0, 4, (hop, last - 1, (late,)), (finish, last - 1, ()))

    @pl.when(jnp.logical_not(edge))
    def _():
        each(2, 4, (hop, last, (early,)))

    each(0, 4, (hop, last, (late,)), (finish, last, ()))

    keep_tok.wait()
    for c in range(len(chunks)):
        cross(c).wait_send()
        swap_hidden(c).wait_send()
        hid_out(c).wait()
        for copy in keep_out(c):
            copy.wait()

        def drain(q, carry, c=c):
            err_out(c, q).wait()
            for d in range(2):
                @pl.when(has_down(d))
                def _():
                    z_copy(c, d, q).wait_send()
            return carry

        lax.fori_loop(0, 4, drain, 0)


def forward_call(slots, tokens, w_gate, w_up, w_down, keep_a, keep_b):
    half, (depth, units) = tokens.shape[0], w_gate.shape
    block = 384 if units % 384 == 0 else 128
    counts = [half * part // 16 for part in (4, 3, 3, 2, 2, 2)]
    chunks = tuple((sum(counts[:i]), count) for i, count in enumerate(counts))
    parts = len(chunks)
    bf, f32 = jnp.bfloat16, jnp.float32
    anywhere = pl.BlockSpec(memory_space=pl.ANY)
    vmem = pl.BlockSpec(memory_space=pltpu.VMEM)
    smem = pl.BlockSpec(memory_space=pltpu.SMEM)
    dma = pltpu.SemaphoreType.DMA
    return pl.pallas_call(
        functools.partial(forward_kernel, chunks, block, slots),
        out_shape=(
            jax.ShapeDtypeStruct((4, half, depth), bf),
            jax.ShapeDtypeStruct((2, half, units), bf),
            jax.ShapeDtypeStruct((half, units), f32),
            jax.ShapeDtypeStruct((half, units), f32),
            jax.ShapeDtypeStruct((2, half, depth), bf),
            jax.ShapeDtypeStruct((2, 8, 128), f32),
            jax.ShapeDtypeStruct((2, 128), jnp.int32),
        ),
        in_specs=[anywhere] * 4 + [smem] * 2,
        out_specs=(anywhere,) * 5 + (vmem,) * 2,
        scratch_shapes=[
            pltpu.VMEM((2, half, depth), bf),
            pltpu.VMEM((2, depth, block), bf),
            pltpu.VMEM((2, depth, block), bf),
            pltpu.VMEM((units, depth), bf),
            pltpu.VMEM((2, half, units), f32),
            pltpu.VMEM((2, 2, half, block), f32),
            pltpu.VMEM((4, 2, half, block), f32),
            pltpu.VMEM((2, half, units), bf),
            pltpu.VMEM((2, half, units), bf),
            pltpu.VMEM((2, half, units), bf),
            pltpu.VMEM((4 * max(counts), units), bf),
            pltpu.VMEM((4 * half, depth), f32),
            pltpu.VMEM((2, 4 * half, depth), bf),
            pltpu.VMEM((2, 4 * half, depth), bf),
            pltpu.VMEM((4 * half, depth), bf),
            pltpu.VMEM((2, units), f32),
            dma, dma, dma((2, 2)), dma, dma((2,)), dma((4,)),
            dma((parts,)), dma((parts,)), dma((parts,)), dma((parts,)),
            dma((parts, 2, 4)), dma((parts, 2, 4)), dma((3, parts)), dma((parts, 4)),
        ],
        compiler_params=pltpu.CompilerParams(
            collective_id=0, has_side_effects=True, vmem_limit_bytes=VMEM_LIMIT
        ),
    )(tokens, w_gate, w_up, w_down, keep_a, keep_b)


def backward_kernel(
    slots,
    plan_ref, err_hbm, wd_hbm, act_hbm, fac_hbm, hid_hbm, sq_ref,
    dga_hbm, dua_hbm, ha_hbm, dgb_hbm, dub_hbm, hb_hbm, loss_ref,
    wd, err, bt, give, got, own, xs, xr, nat, act_t, fac_t, hidb, outs, hout,
    sq_core, sq_chip, sq_all,
    in_s, give_s, give_r, x_s, x_r, own_s, far_s, far_r, h_s, l_s, l_r, z_s, z_r,
):
    n = lax.axis_size("hidden")
    z, wide, core = lax.axis_index("hidden"), lax.axis_index("width"), lax.axis_index("rep")
    units, depth = wd_hbm.shape
    half = act_hbm.shape[0]
    pairs = half // 128
    slots_a, slots_b = slots
    rows_a, rows = slots_a * BLOCK, (slots_a + slots_b) * BLOCK
    partner, across = {"rep": 1 - core}, {"width": 1 - wide}

    def local(src, dst, sem):
        return pltpu.make_async_copy(src, dst, sem)

    def remote(src, dst, ssem, rsem, peer):
        return pltpu.make_async_remote_copy(
            src, dst, ssem, rsem, device_id=peer, device_id_type=MESH
        )

    load_err = local(err_hbm, err, in_s.at[0])
    load_act = local(act_hbm, nat, in_s.at[1])
    load_hid = local(hid_hbm.at[0], hidb, in_s.at[2])
    tile = units // 3

    def load_down(i):
        at = pl.ds(pl.multiple_of(i * tile, 128), tile)
        return local(wd_hbm.at[at], wd.at[at], in_s.at[3 + i])

    load_err.start()
    for i in range(3):
        load_down(i).start()

    barrier = pltpu.get_barrier_semaphore()
    pl.semaphore_signal(barrier, inc=1, device_id=partner, device_id_type=MESH)
    pl.semaphore_signal(barrier, inc=1, device_id=across, device_id_type=MESH)
    for k in range(1, n):
        peer = {"hidden": lax.rem(z + k, n)}
        pl.semaphore_signal(barrier, inc=1, device_id=peer, device_id_type=MESH)
    pl.semaphore_wait(barrier, n + 1)
    loss_core = remote(sq_ref, sq_core, l_s.at[0], l_r.at[0], partner)
    loss_chip = remote(loss_ref, sq_chip, l_s.at[1], l_r.at[1], across)
    loss_core.start()

    def fill(side, p):
        lanes = pl.ds(p * 128, 128)
        rhs = jnp.concatenate([err[side, lanes, :], err[2 + side, lanes, :]], axis=0)

        def piece(i, carry):
            if side == 1 and p == 0:
                load_down(i).wait()
            at = pl.ds(pl.multiple_of(i * tile, 128), tile)
            back = nt(wd[at, :], rhs)
            bt[0, at, :] = back[:, 0:128]
            bt[1, at, :] = back[:, 128:256]
            return carry

        lax.fori_loop(0, 3, piece, 0)

    def per_slot(first, count, action):
        def two(i, carry):
            for k in range(2):
                s = first + 2 * i + k
                base = pl.multiple_of((first + 2 * i) * BLOCK, 8) + k * BLOCK
                action(s, pl.ds(plan_ref[0, s], BLOCK), pl.ds(base, BLOCK))
            return carry

        lax.fori_loop(0, count // 2, two, 0)

    counts = ((0, slots_a), (slots_a, slots_b))
    spans = (pl.ds(0, rows_a), pl.ds(rows_a, rows - rows_a))

    def pick(target, v):
        def take(s, source, place):
            target[place, :] = bt[v, source, :]

        per_slot(*counts[v], take)

    strip = BLOCK * 4

    def strips(v, action):
        base = (0, rows_a)[v]

        def step(i, carry):
            action(pl.ds(pl.multiple_of(base + i * strip, 16), strip))
            return carry

        lax.fori_loop(0, (rows_a, rows - rows_a)[v] // strip, step, 0)

    def push(p, v):
        return remote(
            give.at[p, spans[v]], got.at[p, spans[v]], give_s.at[p, v], give_r.at[p, v], partner
        )

    def cross(p, v):
        return remote(xs.at[p, spans[v]], xr.at[p, spans[v]], x_s.at[p, v], x_r.at[p, v], across)

    load_err.wait()
    for p in range(pairs):
        fill(1, p)
        for v in range(2):
            pick(give.at[p], v)
            push(p, v).start()
        if p == 0:
            load_act.start()
            load_hid.start()
            loss_core.wait()
            loss_ref[...] = sq_ref[...] + sq_core[...]
            loss_chip.start()
        fill(0, p)
        for v in range(2):
            pick(own.at[p], v)
            push(p, v).wait_recv()

            def join(at, p=p):
                total = own[p, at, :] + got[p, at, :]
                own[p, at, :] = total
                xs[p, at, :] = total.astype(jnp.bfloat16)

            strips(v, join)
            cross(p, v).start()

    def flip(source, target, count):
        def step(j, carry):
            lanes = pl.ds(pl.multiple_of(j * 128, 128), 128)
            value = source(lanes).astype(jnp.float32).T.astype(target.dtype)
            if len(target.shape) == 2:
                target[lanes, :] = value
            else:
                for i in range(target.shape[0]):
                    target[i, lanes, :] = value[:, i * 128 : (i + 1) * 128]
            return carry

        lax.fori_loop(0, count // 128, step, 0)

    load_act.wait()
    flip(lambda lanes: nat[:, lanes], act_t, units)
    load_fac = local(fac_hbm, nat, in_s.at[1])
    load_fac.start()
    load_fac.wait()
    flip(lambda lanes: nat[:, lanes], fac_t, units)

    loss_chip.wait()
    sq_all[z] = loss_ref[...] + sq_chip[...]

    def share(k):
        return remote(
            sq_all.at[z], sq_all.at[z], z_s.at[k], z_r.at[z],
            {"hidden": lax.rem(z + k, n)},
        )

    for k in range(1, n):
        share(k).start()

    for p in range(pairs):
        for v in range(2):
            push(p, v).wait_send()

    def keep(s, value):
        return jnp.where(plan_ref[1, s] > 0, value, jnp.zeros_like(value))

    def hid_out(side, p):
        lanes = pl.ds(side * half + p * 128, 128)
        return (
            local(hout.at[side, p, pl.ds(0, rows_a)], ha_hbm.at[:, lanes], h_s.at[0, side, p]),
            local(
                hout.at[side, p, pl.ds(rows_a, rows - rows_a)], hb_hbm.at[:, lanes],
                h_s.at[1, side, p],
            ),
        )

    for side in range(2):
        if side == 0:
            load_hid.wait()
        else:
            next_hid = local(hid_hbm.at[1], hidb, in_s.at[2])
            next_hid.start()
            next_hid.wait()
        flip(lambda lanes: hidb[:, lanes], bt, units)
        for p in range(pairs):
            def copy_rows(s, source, place, p=p):
                give[p, place, :] = keep(s, bt[p, source, :])

            per_slot(0, slots_a + slots_b, copy_rows)

            def narrow(at, p=p, side=side):
                hout[side, p, at, :] = give[p, at, :].astype(jnp.bfloat16)

            for v in range(2):
                strips(v, narrow)
            for copy in hid_out(side, p):
                copy.start()

    def delta_out(p, kind, v):
        near = pl.ds(p * 128, 128)
        far = pl.ds(half + p * 128, 128)
        source = outs.at[p, kind, spans[v]]
        target = ((dga_hbm, dgb_hbm), (dua_hbm, dub_hbm))[kind][v]
        return (
            remote(
                source, target.at[:, far], far_s.at[p, kind, v], far_r.at[p, kind, v], partner
            ),
            local(source, target.at[:, near], own_s.at[p, kind, v]),
        )

    for p in range(pairs):
        for v in range(2):
            cross(p, v).wait_recv()

            def combine(at, p=p):
                own[p, at, :] = own[p, at, :] + xr[p, at, :].astype(jnp.float32)

            strips(v, combine)

            def scale(s, source, place, p=p):
                total = keep(s, own[p, place, :])
                got[0, place, :] = total * fac_t[p, source, :]
                got[1, place, :] = total * act_t[p, source, :]

            per_slot(*counts[v], scale)
            for kind in range(2):
                def narrow(at, p=p, kind=kind):
                    outs[p, kind, at, :] = got[kind, at, :].astype(jnp.bfloat16)

                strips(v, narrow)
                for copy in delta_out(p, kind, v):
                    copy.start()

    total = None
    for i in range(n):
        @pl.when(z != i)
        def _(i=i):
            remote(
                sq_all.at[i], sq_all.at[i], z_s.at[0], z_r.at[i], partner
            ).wait_recv()

    for i in range(n):
        total = sq_all[i] if total is None else total + sq_all[i]
    loss_ref[...] = total

    for k in range(1, n):
        share(k).wait_send()
    for p in range(pairs):
        for v in range(2):
            cross(p, v).wait_send()
            for kind in range(2):
                for copy in delta_out(p, kind, v):
                    copy.wait()
        for side in range(2):
            for copy in hid_out(side, p):
                copy.wait()


def backward_call(plan, slots, err, w_down, act, fac, hid, squares):
    (half, units), depth = act.shape, w_down.shape[1]
    rows_a, rows_b = slots[0] * BLOCK, slots[1] * BLOCK
    rows, pairs, n = rows_a + rows_b, half // 128, lax.axis_size("hidden")
    bf, f32 = jnp.bfloat16, jnp.float32
    anywhere = pl.BlockSpec(memory_space=pl.ANY)
    vmem = pl.BlockSpec(memory_space=pltpu.VMEM)
    smem = pl.BlockSpec(memory_space=pltpu.SMEM)
    dma = pltpu.SemaphoreType.DMA
    shape = jax.ShapeDtypeStruct
    return pl.pallas_call(
        functools.partial(backward_kernel, slots),
        out_shape=(
            (shape((rows_a, 2 * half), bf),) * 3
            + (shape((rows_b, 2 * half), bf),) * 3
            + (shape((2, 8, 128), f32),)
        ),
        in_specs=[smem] + [anywhere] * 5 + [vmem],
        out_specs=(anywhere,) * 6 + (vmem,),
        scratch_shapes=[
            pltpu.VMEM((units, depth), bf),
            pltpu.VMEM((4, half, depth), bf),
            pltpu.VMEM((2, units, 128), f32),
            pltpu.VMEM((pairs, rows, 128), f32),
            pltpu.VMEM((pairs, rows, 128), f32),
            pltpu.VMEM((pairs, rows, 128), f32),
            pltpu.VMEM((pairs, rows, 128), bf),
            pltpu.VMEM((pairs, rows, 128), bf),
            pltpu.VMEM((half, units), f32),
            pltpu.VMEM((pairs, units, 128), f32),
            pltpu.VMEM((pairs, units, 128), f32),
            pltpu.VMEM((half, units), bf),
            pltpu.VMEM((pairs, 2, rows, 128), bf),
            pltpu.VMEM((2, pairs, rows, 128), bf),
            pltpu.VMEM((2, 8, 128), f32),
            pltpu.VMEM((2, 8, 128), f32),
            pltpu.VMEM((n, 2, 8, 128), f32),
            dma((6,)), dma((pairs, 2)), dma((pairs, 2)), dma((pairs, 2)), dma((pairs, 2)),
            dma((pairs, 2, 2)), dma((pairs, 2, 2)), dma((pairs, 2, 2)), dma((2, 2, pairs)),
            dma((2,)), dma((2,)), dma((n,)), dma((n,)),
        ],
        compiler_params=pltpu.CompilerParams(
            collective_id=1, has_side_effects=True, vmem_limit_bytes=VMEM_LIMIT
        ),
    )(plan, err, w_down, act, fac, hid, squares)


def gradient_kernel(
    scale,
    dga, dua, ha, dgb, dub, hb, tok, err, sums_ref,
    gga, gua, gda, ggb, gub, gdb, loss_ref,
    left_a, left_b, right, buffer, in_s, out_s,
):
    pieces = 2
    phases = (
        (dga, left_a.at[0], 0, gga), (dua, left_a.at[1], 0, gua), (ha, left_a.at[2], 1, gda),
        (dgb, left_b.at[0], 0, ggb), (dub, left_b.at[1], 0, gub), (hb, left_b.at[2], 2, gdb),
    )
    sources = [(tok, right.at[0])] + [phase[:2] for phase in phases]
    sources.insert(3, (err.at[0], right.at[1]))
    sources.append((err.at[1], right.at[2]))
    loads = [
        pltpu.make_async_copy(src, dst, in_s.at[i]) for i, (src, dst) in enumerate(sources)
    ]
    for load in loads:
        load.start()
    needs = ((0, 1), (2,), (3, 4), (5,), (6,), (7, 8))

    for k in range(2):
        loss_ref[k] = jnp.sum(sums_ref[k]) * scale
    pending = []
    for (_, left, side, out), which in zip(phases, needs):
        for i in which:
            loads[i].wait()
        rows = left.shape[0] // pieces
        for i in range(pieces):
            slot = len(pending) % 2
            if len(pending) > 1:
                pending[-2].wait()
            at = pl.ds(i * rows, rows)
            buffer[slot, pl.ds(0, rows), :] = nn(left[at, :], right[side]).astype(jnp.bfloat16)
            copy = pltpu.make_async_copy(
                buffer.at[slot, pl.ds(0, rows)], out.at[at], out_s.at[slot]
            )
            copy.start()
            pending.append(copy)
    for copy in pending[-2:]:
        copy.wait()


def gradient_call(scale, dga, dua, ha, dgb, dub, hb, tok, err, sums):
    tokens, depth = tok.shape
    rows_a, rows_b = dga.shape[0], dgb.shape[0]
    bf = jnp.bfloat16
    anywhere = pl.BlockSpec(memory_space=pl.ANY)
    dma = pltpu.SemaphoreType.DMA
    flops = 6 * depth * tokens * (rows_a + rows_b)
    gga, gua, gda, ggb, gub, gdb, losses = pl.pallas_call(
        functools.partial(gradient_kernel, scale),
        out_shape=tuple(
            jax.ShapeDtypeStruct((rows, depth), bf) for rows in (rows_a,) * 3 + (rows_b,) * 3
        ) + (jax.ShapeDtypeStruct((2,), jnp.float32),),
        in_specs=[anywhere] * 8 + [pl.BlockSpec(memory_space=pltpu.VMEM)],
        out_specs=(anywhere,) * 6 + (pl.BlockSpec(memory_space=pltpu.SMEM),),
        scratch_shapes=[
            pltpu.VMEM((3, rows_a, tokens), bf),
            pltpu.VMEM((3, rows_b, tokens), bf),
            pltpu.VMEM((3, tokens, depth), bf),
            pltpu.VMEM((2, rows_a // 2, depth), bf),
            dma((9,)), dma((2,)),
        ],
        compiler_params=pltpu.CompilerParams(vmem_limit_bytes=VMEM_LIMIT),
        cost_estimate=pl.CostEstimate(
            flops=flops, bytes_accessed=4 * depth * (rows_a + rows_b) * 2, transcendentals=0
        ),
    )(dga, dua, ha, dgb, dub, hb, tok, err, sums)
    return gga.T, gua.T, gda, ggb.T, gub.T, gdb, losses


def per_device_fast(tokens, w_gate, w_up, w_down, keep_a, keep_b):
    shard_blocks = keep_a.shape[0]
    slots = (3 * shard_blocks // 4, shard_blocks // 2)
    err, hid, act, fac, tok, squares, plan = forward_call(
        slots, tokens, w_gate, w_up, w_down, keep_a, keep_b
    )
    *deltas, sums = backward_call(plan, slots, err, w_down, act, fac, hid, squares)
    token_count = 2 * tokens.shape[0]
    scale = 1.0 / (lax.axis_size("hidden") * token_count * D)
    return gradient_call(
        scale, *deltas, tok.reshape(token_count, -1), err.reshape(2, token_count, -1), sums
    )


def solution(mesh):
    in_specs = (
        P(("groups", "rep"), "width"),
        P(("width", "rep"), "hidden"),
        P(("width", "rep"), "hidden"),
        P("hidden", ("width", "rep")),
        P("hidden"),
        P("hidden"),
    )
    out_specs = (
        P(("width", "rep"), ("groups", "hidden")),
        P(("width", "rep"), ("groups", "hidden")),
        P(("groups", "hidden"), ("width", "rep")),
        P(("width", "rep"), ("groups", "hidden")),
        P(("width", "rep"), ("groups", "hidden")),
        P(("groups", "hidden"), ("width", "rep")),
        P("groups"),
    )
    sizes = mesh.shape
    body = per_device
    if sizes["width"] == 2 and sizes["rep"] == 2 and 2 <= sizes["hidden"] <= 4:
        body = per_device_fast
    return jax.shard_map(
        body, mesh=mesh, in_specs=in_specs, out_specs=out_specs, check_vma=False
    )
```
